32 devices in a mesh: groups: 2 (over x), seq: 16 (over z, y, core).
Axes of the slice: x: 2, y: 2, z: 4, core: 2. Of those that a mesh axis runs over, the one named last changes fastest.
Arguments:
- patches: bfloat16 [4096, 1176], P(('groups', 'seq')), parts along dimension 0, may hold values from -6 to 6
- row_owner: int32 [4096, 1], P(('groups', 'seq')), parts along dimension 0, may hold values from 0 to 15; in each aligned block of 128 rows (0 to 127, 128 to 255, ...) at most 16 rows name the same one
- window_slot: int32 [4096], P(('groups', 'seq')), parts along dimension 0, may hold values from 0 to 3
- w_patch: bfloat16 [1176, 1280], replicated, may hold values from -1 to 1
- vit_gain: float32 [1280], replicated, may hold values from 0.1 to 1.9
- w_qkv: bfloat16 [1280, 1920], replicated, may hold values from -1 to 1
- queries: bfloat16 [4096, 4096], P(('groups', 'seq')), parts along dimension 0, may hold values from -36 to 36
- new_kv: bfloat16 [4096, 1024], P(('groups', 'seq')), parts along dimension 0, may hold values from -6 to 6
- kv_cache: bfloat16 [2048, 16, 1024], P(('groups', 'seq')), parts along dimension 0, may hold values from -6 to 6
- block_table: int32 [32, 64], P(('groups', 'seq')), parts along dimension 0, may hold values from -1 to 1023, as said below
Outputs:
- vision_out: bfloat16 [4096, 640], P(('groups', 'seq')), parts along dimension 0
- attention_out: bfloat16 [4096, 4096], P(('groups', 'seq')), parts along dimension 0
The draws below stay inside these ranges and needn't reach their ends.
There are 2 independent parts, one for each index of `groups`. The reference program is written for one: setup_inputs(seed, part) draws one part's arguments, and reference() takes and returns one part's arrays. A program takes and returns all parts, laid end to end along the dimension named above; an argument that names none is the same for every part. Nothing has to cross between parts.
Inputs may be any that keep to these rules, and one draw needn't show every extreme that they name: `row_owner`: in the rows of one device, each owner is named by at most 16 rows. `block_table`: block b is stored on device b // 64. Each row lists 8 or more distinct blocks, then -1 entries; at most 8 of a row's blocks lie on one device.
All inputs are finite; a program needn't handle non-finite values.
Results may differ from the reference program's by a relative error of at most 0.0093.
Values may be sent and summed in bfloat16 or wider, within the bound.
A program may use at most 64 MiB of HBM per device.

```python
import math
import jax
import jax.numpy as jnp
import numpy as np
from jax import lax

SRC_ROWS = 128
ROWS = 2048
CAP = 16
PATCH = 1176
VIT = 1280
VHEADS = 8
VHD = 80
VQKV = 640
WSLOTS = 4
TOK_DEV = 128
TOKENS = 2048
QHEADS = 32
KVH = 4
HD = 128
BT = 16
BLK_DEV = 64
TMAX = 64
N_SEQ = 16


def table_law(key):
    table_key = jax.random.fold_in(key, 101)
    star_key, perm_key, offset_key, length_key, longest_key = jax.random.split(table_key, 5)
    per_owner = 2 * TMAX // N_SEQ
    star_owner = jax.random.randint(star_key, (), 0, N_SEQ)
    reader_keys = jax.random.split(perm_key, N_SEQ)
    rest_owner = jax.vmap(lambda sub_key: jax.random.permutation(sub_key, N_SEQ - 1))(reader_keys) + 1
    owner_order = jnp.concatenate([jnp.zeros((N_SEQ, 1), jnp.int32), rest_owner.astype(jnp.int32)], axis=1)
    owners_all = (star_owner + owner_order) % N_SEQ
    slot_index = jnp.arange(TMAX)
    owner_entry = owners_all[:, slot_index // per_owner]
    offsets = jax.random.randint(offset_key, (N_SEQ, N_SEQ), 0, BLK_DEV)
    local_index = (jnp.take_along_axis(offsets, owner_entry, axis=1) + slot_index[None, :] % per_owner) % BLK_DEV
    lengths = jax.random.randint(length_key, (N_SEQ,), per_owner, TMAX + 1)
    longest = jax.random.randint(longest_key, (), 0, N_SEQ)
    lengths = jnp.where(jnp.arange(N_SEQ) == longest, TMAX, lengths)
    entries = owner_entry * BLK_DEV + local_index
    return jnp.where(slot_index[None, :] < lengths[:, None], entries, -1).astype(jnp.int32)


def cache_law(key):
    cache_key = jax.random.fold_in(key, 202)
    array_shape = (N_SEQ * BLK_DEV, BT, 2 * KVH * HD)
    values = jnp.clip(jax.random.normal(cache_key, array_shape, jnp.float32), -6.0, 6.0)
    return values


def draw_block_table(key, part):
    return table_law(key)


def draw_kv_cache(key, part):
    return cache_law(key).astype(jnp.bfloat16)


def draw_queries(key, part):
    query_key = jax.random.fold_in(key, 303)
    array_shape = (N_SEQ * TOK_DEV, QHEADS * HD)
    values = jnp.clip(jax.random.normal(query_key, array_shape, jnp.float32), -6.0, 6.0)
    return values.astype(jnp.bfloat16)


def draw_patches(key, part):
    patch_key = jax.random.fold_in(key, 707)
    row_count = N_SEQ * SRC_ROWS
    array_shape = (row_count, PATCH)
    values = jnp.clip(jax.random.normal(patch_key, array_shape, jnp.float32), -6.0, 6.0)
    return values.astype(jnp.bfloat16)


def draw_w_patch(key, part):
    weight_key = jax.random.fold_in(key, 505)
    array_shape = (PATCH, VIT)
    values = jnp.clip(jax.random.normal(weight_key, array_shape, jnp.float32), -6.0, 6.0) * PATCH ** (-0.5)
    return values.astype(jnp.bfloat16)


def draw_w_qkv(key, part):
    weight_key = jax.random.fold_in(key, 606)
    inner_width = VHEADS * VHD
    array_shape = (VIT, 3 * inner_width)
    values = jnp.clip(jax.random.normal(weight_key, array_shape, jnp.float32), -6.0, 6.0) * VIT ** (-0.5)
    return values.astype(jnp.bfloat16)


def place_ends(values, stream_key, low, top_value):
    longest = values.shape.index(max(values.shape))
    spots = []
    for shift in (0, 1):
        where = [jax.random.randint(jax.random.fold_in(stream_key, axis), (), 0, length) for axis, length in enumerate(values.shape)]
        where[longest] = (where[longest] + shift) % values.shape[longest]
        spots.append(tuple(where))
    return values.at[spots[0]].set(low).at[spots[1]].set(top_value)


def steps_of(rng, dims, shards, low, top_value):
    def one(position, parts):
        draws = jax.random.uniform(jax.random.fold_in(jax.random.fold_in(rng, 6), position), (parts,), jnp.float32, low / len(shards), top_value / len(shards))
        return jnp.repeat(jnp.exp(draws), dims[position] // parts).reshape((-1,) + (1,) * (len(dims) - position - 1))

    loudness = one(*shards[0])
    for cut in shards[1:]:
        loudness = loudness * one(*cut)
    return loudness


def assign_block(rng, own, number, rows, amount, top, limit, slope):
    ranking = jax.random.permutation(rng, amount)
    crowded, usual = portions_of(amount, rows * top, limit, slope, True), portions_of(amount, rows * top, limit, slope, False)
    places = jnp.arange(amount)

    def named(sizes, rotation):
        used = int((sizes > 0).sum())
        fixed = max(1, used // 4)
        passed = fixed + (places - fixed + rotation * (used - fixed)) % max(1, amount - fixed)
        return jnp.zeros((amount,), jnp.int32).at[ranking[jnp.where(places < fixed, places, passed)]].set(jnp.asarray(sizes, jnp.int32))

    sizes = jnp.where(number % 4 == 0, named(crowded, number // 4), named(usual, number - number // 4 - 1))
    mixed = jax.random.permutation(jax.random.fold_in(own, 3), amount)
    giver, receiver = mixed[0:amount // 2 * 2:2], mixed[1:amount // 2 * 2:2]
    room = jnp.minimum(sizes[giver] - 1, limit - sizes[receiver]) // 2
    room = jnp.where((giver == ranking[0]) | (receiver == ranking[0]) | (sizes[receiver] == 0), 0, jnp.maximum(room, 0))
    passed = jax.random.randint(jax.random.fold_in(own, 4), (amount // 2,), 0, 1 << 20) % (room + 1)
    sizes = sizes.at[giver].add(-passed).at[receiver].add(passed)
    labels = jnp.searchsorted(jnp.cumsum(sizes), jnp.arange(rows * top), side="right").astype(jnp.int32)
    table = labels.reshape(top, rows).T
    table = table[jax.random.permutation(jax.random.fold_in(own, 1), rows)]
    rotation = jax.random.randint(jax.random.fold_in(own, 2), (rows, 1), 0, top)
    return jnp.take_along_axis(table, (jnp.arange(top)[None, :] + rotation) % top, axis=1)


def portions_of(count, total, reach, skew, full):
    portions = [(1 << 20) // math.isqrt(standing ** skew) + 1 for standing in range(1, count + 1)]
    largest = reach if full else min(reach, max(-(-total // count), total * portions[0] // sum(portions)))
    least = 1 if total - largest >= count - 1 else 0
    counts, surplus = [largest] + [least] * (count - 1), total - largest - least * (count - 1)
    while surplus > 0:
        movable = [i for i in range(1, count) if counts[i] < largest] or [i for i in range(1, count) if counts[i] < reach]
        whole, remaining = sum([portions[i] for i in movable]), surplus
        for i in movable:
            extra = min(reach - counts[i], max(1, remaining * portions[i] // whole), surplus)
            counts[i] = counts[i] + extra
            surplus = surplus - extra
    return np.array(counts)


def bell_draw(stream_key, shape, deviation, reach, cuts=(), kind=jnp.bfloat16):
    values = deviation * jax.random.normal(stream_key, shape, jnp.float32)
    if cuts:
        values = values * steps_of(stream_key, shape, cuts, -0.22, 0.18)
    return jnp.clip(values, -reach, reach).astype(kind)


def setup_inputs(seed: int = 0, part: int = 0) -> dict:
    keys = jax.random.split(jax.random.key(seed), 11)
    own_keys = jax.random.split(jax.random.fold_in(keys[10], part), 11)
    patches = draw_patches(jax.random.fold_in(jax.random.fold_in(keys[10], part), 71), part)
    row_owner_keys = jax.random.split(jax.random.fold_in(own_keys[1], 1), ROWS // SRC_ROWS)
    row_owner_turns = jax.random.permutation(jax.random.fold_in(own_keys[1], 3), ROWS // SRC_ROWS)
    row_owner = jax.vmap(lambda own, number: assign_block(jax.random.fold_in(own_keys[1], 2), own, number, SRC_ROWS, N_SEQ, 1, CAP, 2))(row_owner_keys, row_owner_turns).reshape((ROWS, 1))
    window_slot = place_ends(jax.random.randint(own_keys[2], (ROWS,), 0, WSLOTS), jax.random.fold_in(own_keys[2], 1), 0, WSLOTS - 1).astype(jnp.int32)
    w_patch = draw_w_patch(jax.random.fold_in(keys[10], 71), part)
    vit_gain = jnp.clip(1.0 + 0.18 * jax.random.normal(keys[4], (VIT,), jnp.float32), 0.1, 1.9)
    w_qkv = draw_w_qkv(jax.random.fold_in(keys[10], 71), part)
    queries = draw_queries(jax.random.fold_in(jax.random.fold_in(keys[10], part), 71), part)
    new_kv = bell_draw(own_keys[7], (TOKENS, 2 * KVH * HD), 1.0, 6.0, ((0, 16),))
    kv_cache = draw_kv_cache(jax.random.fold_in(jax.random.fold_in(keys[10], part), 71), part)
    block_table = draw_block_table(jax.random.fold_in(jax.random.fold_in(keys[10], part), 71), part)
    return dict(patches=patches, row_owner=row_owner, window_slot=window_slot, w_patch=w_patch, vit_gain=vit_gain, w_qkv=w_qkv, queries=queries, new_kv=new_kv, kv_cache=kv_cache, block_table=block_table)


def embed_rows(patch_rows, w_patch, vit_gain):
    embedded = jnp.dot(patch_rows, w_patch, preferred_element_type=jnp.float32).astype(jnp.bfloat16)
    widened = lax.optimization_barrier(embedded).astype(jnp.float32)
    factor = lax.rsqrt(lax.optimization_barrier(jnp.mean(widened * widened, axis=1, keepdims=True)) + 1e-06)
    return (widened * factor * vit_gain).astype(jnp.bfloat16)

def window_attention(qkv_rows, windows):
    total_rows = qkv_rows.shape[0]
    inner_width = VHEADS * VHD
    query_heads = qkv_rows[:, :inner_width].reshape(total_rows, VHEADS, VHD).astype(jnp.float32)
    key_heads = qkv_rows[:, inner_width:2 * inner_width].reshape(total_rows, VHEADS, VHD).astype(jnp.float32)
    value_heads = qkv_rows[:, 2 * inner_width:].reshape(total_rows, VHEADS, VHD).astype(jnp.float32)
    is_live = windows >= 0
    scores = jnp.einsum('qhd,khd->hqk', query_heads, key_heads) * VHD ** (-0.5)
    row_index = jnp.arange(total_rows)
    allowed = (windows[:, None] == windows[None, :]) & is_live[None, :] | (row_index[:, None] == row_index[None, :])
    scores = jnp.where(allowed[None], scores, -jnp.inf)
    highest = lax.optimization_barrier(jnp.max(scores, axis=2, keepdims=True))
    weights = jnp.exp(scores - highest)
    totals = lax.optimization_barrier(jnp.sum(weights, axis=2))
    rounded = lax.optimization_barrier(weights.astype(jnp.bfloat16)).astype(jnp.float32)
    blended = jnp.einsum('hqk,khd->qhd', rounded, value_heads)
    return (blended / totals.T[:, :, None]).reshape(total_rows, inner_width).astype(jnp.bfloat16)

def prompt_attention(query_rows, fresh_kv, cached_kv, cached_live):
    token_count = query_rows.shape[0]
    kv_width = KVH * HD
    group_size = QHEADS // KVH
    every_kv = jnp.concatenate([cached_kv, fresh_kv], axis=0).astype(jnp.float32)
    causal = jnp.arange(token_count)[None, :] <= jnp.arange(token_count)[:, None]
    allowed = jnp.concatenate([jnp.broadcast_to(cached_live[None, :], (token_count, cached_live.shape[0])), causal], axis=1)
    outputs = []
    for head_group in range(KVH):
        query_heads = query_rows[:, head_group * group_size * HD:(head_group + 1) * group_size * HD]
        query_heads = query_heads.reshape(token_count, group_size, HD).astype(jnp.float32)
        key_head = every_kv[:, head_group * HD:(head_group + 1) * HD]
        value_head = every_kv[:, kv_width + head_group * HD:kv_width + (head_group + 1) * HD]
        scores = jnp.einsum('cpd,kd->cpk', query_heads, key_head) * HD ** (-0.5)
        scores = jnp.where(allowed[:, None, :], scores, -jnp.inf)
        highest = lax.optimization_barrier(jnp.max(scores, axis=2, keepdims=True))
        weights = jnp.exp(scores - highest)
        totals = lax.optimization_barrier(jnp.sum(weights, axis=2))
        rounded = lax.optimization_barrier(weights.astype(jnp.bfloat16)).astype(jnp.float32)
        blended = jnp.einsum('cpk,kd->cpd', rounded, value_head)
        outputs.append((blended / totals[:, :, None]).reshape(token_count, group_size * HD))
    return jnp.concatenate(outputs, axis=1).astype(jnp.bfloat16)

def reference(patches, row_owner, window_slot, w_patch, vit_gain, w_qkv, queries, new_kv, kv_cache, block_table):
    normed = embed_rows(patches, w_patch, vit_gain)
    qkv_all = jnp.dot(normed, w_qkv, preferred_element_type=jnp.float32).astype(jnp.bfloat16)
    owner_ids = row_owner[:, 0]
    slot_count = 2 * SRC_ROWS

    def per_owner(owner):
        picked = jnp.nonzero(owner_ids == owner, size=slot_count, fill_value=ROWS)[0].astype(jnp.int32)
        is_live = picked < ROWS
        safe_rows = jnp.minimum(picked, ROWS - 1)
        windows = jnp.where(is_live, window_slot[safe_rows], -1)
        return (window_attention(qkv_all[safe_rows], windows), picked)
    attended, picked_rows = lax.map(per_owner, jnp.arange(N_SEQ, dtype=jnp.int32))
    vision_out = jnp.zeros((ROWS, VQKV), jnp.bfloat16).at[picked_rows.reshape(-1)].set(attended.reshape(-1, VQKV), mode='drop')

    def per_reader(reader):
        table_row = block_table[reader]
        is_live = table_row >= 0
        blocks = kv_cache[jnp.maximum(table_row, 0)]
        cached_kv = blocks.reshape(TMAX * BT, 2 * KVH * HD)
        cached_live = jnp.repeat(is_live, BT)
        first_row = (reader * TOK_DEV).astype(jnp.int32)
        query_rows = lax.dynamic_slice_in_dim(queries, first_row, TOK_DEV, 0)
        fresh_kv = lax.dynamic_slice_in_dim(new_kv, first_row, TOK_DEV, 0)
        return prompt_attention(query_rows, fresh_kv, cached_kv, cached_live)
    attention_out = lax.map(per_reader, jnp.arange(N_SEQ, dtype=jnp.int32)).reshape(TOKENS, QHEADS * HD)
    return (vision_out, attention_out)
```

```python
import functools

import jax
import jax.numpy as jnp
from jax import lax
from jax.experimental import pallas as pl
from jax.experimental.pallas import tpu as pltpu
from jax.sharding import PartitionSpec as P

VHEADS = 8
VHD = 80
QHEADS = 32
KVH = 4
HD = 128
DEAD = -1e30


def embed_rows(patch_rows, w_patch, vit_gain):
    embedded = jnp.dot(patch_rows, w_patch, preferred_element_type=jnp.float32).astype(jnp.bfloat16)
    widened = lax.optimization_barrier(embedded).astype(jnp.float32)
    factor = lax.rsqrt(jnp.mean(widened * widened, axis=1, keepdims=True) + 1e-06)
    return (widened * factor * vit_gain).astype(jnp.bfloat16)


def window_attention(qkv_rows, windows):
    total_rows = qkv_rows.shape[0]
    inner_width = VHEADS * VHD
    query_heads = qkv_rows[:, :inner_width].reshape(total_rows, VHEADS, VHD)
    key_heads = qkv_rows[:, inner_width : 2 * inner_width].reshape(total_rows, VHEADS, VHD)
    value_heads = qkv_rows[:, 2 * inner_width :].reshape(total_rows, VHEADS, VHD)
    is_live = windows >= 0
    every_row = jnp.arange(total_rows)
    scores = jnp.einsum(
        "qhd,khd->hqk", query_heads, key_heads, preferred_element_type=jnp.float32
    ) * VHD ** (-0.5)
    allowed = (windows[:, None] == windows[None, :]) & is_live[None, :] | (
        every_row[:, None] == every_row[None, :]
    )
    scores = jnp.where(allowed[None], scores, -jnp.inf)
    highest = jnp.max(scores, axis=2, keepdims=True)
    weights = jnp.exp(scores - highest)
    totals = jnp.sum(weights, axis=2)
    blended = jnp.einsum(
        "hqk,khd->qhd",
        weights.astype(jnp.bfloat16),
        value_heads,
        preferred_element_type=jnp.float32,
    )
    pieces = (blended / totals.T[:, :, None]).reshape(total_rows, inner_width)
    return pieces.astype(jnp.bfloat16)


def span_kernel(slots, q_ref, fresh_ref, bias_ref, kv_ref, o_ref, held, sems):
    tokens = q_ref.shape[0]
    table_len, block_tokens = held.shape[0] - tokens // kv_ref.shape[1], kv_ref.shape[1]
    group_size = QHEADS // KVH
    width = held.shape[2]

    def copy_of(t):
        return pltpu.make_async_copy(kv_ref.at[slots[t]], held.at[t], sems.at[t])

    fresh_copy = pltpu.make_async_copy(
        fresh_ref, held.at[pl.ds(table_len, tokens // block_tokens)], sems.at[table_len]
    )
    fresh_copy.start()
    for t in range(table_len):
        copy_of(t).start()
    for t in range(table_len):
        copy_of(t).wait()
    fresh_copy.wait()
    keys = held.shape[0] * block_tokens
    rows = 2 * tokens
    causal = lax.broadcasted_iota(jnp.int32, (rows, keys), 1) - table_len * block_tokens <= lax.rem(
        lax.broadcasted_iota(jnp.int32, (rows, keys), 0), tokens
    )
    bias = jnp.where(causal, bias_ref[...], DEAD)
    for g in range(KVH):
        key_head = held[:, :, g * HD : (g + 1) * HD].reshape(keys, HD)
        value_head = held[:, :, width // 2 + g * HD : width // 2 + (g + 1) * HD].reshape(keys, HD)
        for pair in range(group_size // 2):
            first = g * group_size + 2 * pair
            query = jnp.concatenate(
                [q_ref[:, (first + i) * HD : (first + i + 1) * HD] for i in range(2)], axis=0
            )
            scores = lax.dot_general(
                query, key_head, (((1,), (1,)), ((), ())), preferred_element_type=jnp.float32
            ) * HD ** (-0.5) + bias
            highest = jnp.max(scores, axis=1, keepdims=True)
            weights = jnp.exp(scores - highest)
            totals = jnp.sum(weights, axis=1, keepdims=True)
            blended = jnp.dot(
                weights.astype(jnp.bfloat16), value_head, preferred_element_type=jnp.float32
            )
            out = (blended / totals).astype(jnp.bfloat16)
            for i in range(2):
                o_ref[:, (first + i) * HD : (first + i + 1) * HD] = out[i * tokens : (i + 1) * tokens]


def prompt_attention(queries, new_kv, delivered, slots, table_live):
    tokens = queries.shape[0]
    table_len = slots.shape[0]
    block_tokens, width = delivered.shape[1:]
    held_blocks = table_len + tokens // block_tokens
    bias = jnp.concatenate(
        [
            jnp.where(jnp.repeat(table_live, block_tokens), 0.0, DEAD),
            jnp.zeros((tokens,), jnp.float32),
        ]
    ).astype(jnp.float32)[None, :]
    return pl.pallas_call(
        span_kernel,
        out_shape=jax.ShapeDtypeStruct(queries.shape, jnp.bfloat16),
        grid_spec=pltpu.PrefetchScalarGridSpec(
            num_scalar_prefetch=1,
            in_specs=[
                pl.BlockSpec(memory_space=pltpu.VMEM),
                pl.BlockSpec(memory_space=pl.ANY),
                pl.BlockSpec(memory_space=pltpu.VMEM),
                pl.BlockSpec(memory_space=pl.ANY),
            ],
            out_specs=pl.BlockSpec(memory_space=pltpu.VMEM),
            scratch_shapes=[
                pltpu.VMEM((held_blocks, block_tokens, width), jnp.bfloat16),
                pltpu.SemaphoreType.DMA((table_len + 1,)),
            ],
        ),
        compiler_params=pltpu.CompilerParams(vmem_limit_bytes=40 << 20),
        name="span",
    )(slots, queries, new_kv.reshape(tokens // block_tokens, block_tokens, width), bias, delivered)


def route_kernel(
    devices,
    scale_dims,
    patches_hbm,
    owner_ref,
    window_ref,
    w_patch_hbm,
    gain_ref,
    w_qkv_hbm,
    queries_hbm,
    fresh_hbm,
    cache_hbm,
    table_ref,
    vision_ref,
    span_ref,
    patches,
    w_patch,
    w_qkv,
    cache,
    query,
    fresh,
    notes,
    picks,
    picks_smem,
    staged,
    spans,
    span_bias,
    own_query,
    vision_kv,
    pieces,
    top,
    total,
    blend,
    load_sems,
    query_sems,
    pick_sem,
    note_send,
    note_recv,
    patch_send,
    patch_recv,
    span_send,
    span_recv,
):
    vit, blocks_dev, block_tokens, per_owner = scale_dims
    me = lax.axis_index("seq")
    tokens = fresh.shape[0]
    src_rows = owner_ref.shape[1]
    chunk = per_owner * block_tokens
    inner = VHEADS * VHD
    group_rows = QHEADS // KVH * tokens
    kv_width = KVH * HD
    half = devices // 2
    bits = devices.bit_length() - 1

    def peer(k):
        other = me
        bit = 1
        while bit < devices:
            other = other + bit * ((k // bit) % 2) * (1 - 2 * ((me // bit) % 2))
            bit *= 2
        return other

    def remote(src, dst, send, recv, i, k):
        return pltpu.make_async_remote_copy(
            src_ref=src,
            dst_ref=dst,
            send_sem=send.at[i],
            recv_sem=recv.at[i],
            device_id={"seq": peer(k)},
            device_id_type=pl.DeviceIdType.MESH,
        )

    def note_copy(k):
        return remote(notes.at[0], notes.at[k], note_send, note_recv, k, k)

    def patch_copy(place):
        step = place.bit_length() - 1
        return remote(
            patches.at[place - (1 << step)],
            patches.at[place],
            patch_send,
            patch_recv,
            place,
            devices >> (step + 1),
        )

    def forward(place):
        step = place.bit_length()
        while (1 << step) < devices:
            patch_copy(place + (1 << step)).start()
            step += 1

    def take(place):
        patch_copy(place).wait_recv()
        forward(place)

    def span_copy(k):
        base = k * chunk
        rows = pl.ds(base if isinstance(k, int) else pl.multiple_of(base, chunk), chunk)
        return remote(staged.at[rows], spans.at[rows], span_send, span_recv, k, k)

    others = range(1, devices)
    notes[0, 0:per_owner] = jnp.concatenate(
        [
            jnp.broadcast_to(table_ref[...], (per_owner, table_ref.shape[1])),
            jnp.full((per_owner, HD - table_ref.shape[1]), -1, jnp.int32),
        ],
        axis=1,
    )
    window_ids = window_ref[...] * devices + owner_ref[...]
    notes[0, per_owner:] = jnp.broadcast_to(window_ids, (per_owner, src_rows))
    pairs = (
        (patches_hbm, patches.at[0]),
        (cache_hbm, cache),
        (fresh_hbm, fresh),
        (w_patch_hbm, w_patch),
        (w_qkv_hbm, w_qkv),
    )
    loads = [pltpu.make_async_copy(a, b, load_sems.at[i]) for i, (a, b) in enumerate(pairs)]
    query_loads = [
        pltpu.make_async_copy(
            queries_hbm.at[:, pl.ds(h * HD, HD)],
            query.at[pl.ds(h * tokens, tokens)],
            query_sems.at[h],
        )
        for h in range(QHEADS)
    ]
    for load in loads[:3] + query_loads + loads[3:]:
        load.start()

    barrier = pltpu.get_barrier_semaphore()
    for k in others:
        pl.semaphore_signal(
            barrier, inc=1, device_id={"seq": peer(k)}, device_id_type=pl.DeviceIdType.MESH
        )
    pl.semaphore_wait(barrier, devices - 1)
    for k in reversed(others):
        note_copy(k).start()
    loads[0].wait()
    forward(0)

    for k in others:
        note_copy(k).wait()
    asked = notes[:, 0:per_owner].reshape(devices * per_owner, HD)
    first = me * blocks_dev
    hits = (asked >= first) & (asked < first + blocks_dev)
    before = (
        lax.broadcasted_iota(jnp.int32, (HD, HD), 0) < lax.broadcasted_iota(jnp.int32, (HD, HD), 1)
    )
    places = jnp.dot(
        jnp.where(hits, 1.0, 0.0).astype(jnp.bfloat16),
        jnp.where(before, 1.0, 0.0).astype(jnp.bfloat16),
        preferred_element_type=jnp.float32,
    ).astype(jnp.int32)
    turn = lax.rem(lax.broadcasted_iota(jnp.int32, asked.shape, 0), per_owner)
    local = jnp.sum(
        jnp.where(hits & (places == turn), (asked - first).astype(jnp.float32), 0.0),
        axis=1,
        keepdims=True,
    ).astype(jnp.int32)
    picks[...] = jnp.broadcast_to(local, picks.shape)
    pick_copy = pltpu.make_async_copy(picks, picks_smem, pick_sem)
    pick_copy.start()
    loads[1].wait()
    pick_copy.wait()

    def gather(k):
        target = staged if k else spans
        for s in range(per_owner):
            pick = jnp.clip(picks_smem[k * per_owner + s, 0], 0, blocks_dev - 1)
            target[pl.ds(k * chunk + s * block_tokens, block_tokens), :] = cache[pick]

    far, near = list(range(half, devices)), list(range(1, half))
    for k in far[:2]:
        gather(k)
        span_copy(k).start()
    for k in far[2:] + near + [0]:
        gather(k)
    own = notes[0, 0:per_owner]
    step = lax.broadcasted_iota(jnp.int32, (per_owner, HD), 1)
    for k in range(devices):
        first = peer(k) * blocks_dev
        mine = (own >= first) & (own < first + blocks_dev)
        count = jnp.sum(jnp.where(mine, 1.0, 0.0), axis=1, keepdims=True).astype(jnp.int32)
        span_bias[k] = jnp.where(step < count * block_tokens, 0.0, DEAD)

    flip = (((0,), (0,)), ((), ()))
    contract = (((1,), (1,)), ((), ()))
    loads[2].wait()
    for load in query_loads:
        load.wait()
    causal = lax.rem(
        lax.broadcasted_iota(jnp.int32, (group_rows, tokens), 0), tokens
    ) >= lax.broadcasted_iota(jnp.int32, (group_rows, tokens), 1)
    for g in range(KVH):
        rows = slice(g * group_rows, (g + 1) * group_rows)
        scores = lax.dot_general(
            query[rows], fresh[:, g * HD : (g + 1) * HD], contract, preferred_element_type=jnp.float32
        ) * HD ** (-0.5)
        scores = jnp.where(causal, scores, DEAD)
        highest = jnp.max(scores, axis=1, keepdims=True)
        weights = jnp.exp(scores - highest)
        top[rows] = jnp.broadcast_to(highest, (group_rows, HD))
        total[rows] = weights
        blend[rows] = jnp.dot(
            weights.astype(jnp.bfloat16),
            fresh[:, kv_width + g * HD : kv_width + (g + 1) * HD],
            preferred_element_type=jnp.float32,
        )

    def near_places(offset):
        return [p for p in range(devices) if p % 2 == offset]

    for place in near_places(0)[1:]:
        take(place)
    take(1)
    for k in far[2:] + near[::-1]:
        span_copy(k).start()

    def embed(i, _):
        place = 0
        for b in range(bits - 1):
            place = place + ((i // (1 << b)) % 2) * (1 << (bits - 2 - b))
        rows = jnp.concatenate([patches[place], patches[place + half]], axis=1)
        embedded = (
            lax.dot_general(rows, w_patch[...], flip, preferred_element_type=jnp.float32)
            .astype(jnp.bfloat16)
            .astype(jnp.float32)
        )
        factor = lax.rsqrt(jnp.mean(embedded * embedded, axis=1, keepdims=True) + 1e-06)
        normed = (embedded * factor * gain_ref[...].reshape(1, vit)).astype(jnp.bfloat16)
        vision_kv[pl.ds(pl.multiple_of(i * 2 * src_rows, 2 * src_rows), 2 * src_rows), :] = jnp.dot(
            normed, w_qkv[:, inner:], preferred_element_type=jnp.float32
        ).astype(jnp.bfloat16)

        @pl.when(i == 0)
        def _():
            own_query[...] = jnp.dot(
                normed[0:src_rows], w_qkv[:, 0:inner], preferred_element_type=jnp.float32
            ).astype(jnp.bfloat16)

        return 0

    def absorb(k, width):
        base = k * chunk
        bias = jnp.concatenate([span_bias[k + i, 0:1] for i in range(width)], axis=1)
        span = pl.ds(pl.multiple_of(base, chunk), width * chunk)
        for g in range(KVH):
            rows = slice(g * group_rows, (g + 1) * group_rows)
            scores = lax.dot_general(
                query[rows],
                spans[span, g * HD : (g + 1) * HD],
                contract,
                preferred_element_type=jnp.float32,
            ) * HD ** (-0.5) + bias
            old = top[rows]
            highest = jnp.maximum(old, jnp.max(scores, axis=1, keepdims=True))
            shrink = jnp.exp(old - highest)
            parts = [
                jnp.exp(scores[:, i * chunk : (i + 1) * chunk] - highest) for i in range(width)
            ]
            summed = total[rows] * shrink
            for part in parts:
                summed = summed + part
            weights = jnp.concatenate([part.astype(jnp.bfloat16) for part in parts], axis=1)
            top[rows] = highest
            total[rows] = summed
            blend[rows] = blend[rows] * shrink + jnp.dot(
                weights,
                spans[span, kv_width + g * HD : kv_width + (g + 1) * HD],
                preferred_element_type=jnp.float32,
            )

    quarter = me // (devices // 4)
    outer = (quarter == 0) | (quarter == 3)
    block = devices // 8

    def pair_at(j):
        third = j // block
        moved = jnp.where(
            outer,
            jnp.where(third == 1, 1, jnp.where(third == 2, 3, 2)),
            jnp.where(third == 1, 2, jnp.where(third == 2, 1, 3)),
        )
        return 2 * (jnp.where(third == 0, 0, moved) * block + j % block)

    def absorb_pair(j, _):
        k = pair_at(j)
        span_copy(k).wait_recv()
        span_copy(k + 1).wait_recv()
        absorb(k, 2)
        return 0

    loads[3].wait()
    loads[4].wait()
    lax.fori_loop(0, half // 2, embed, 0)
    span_copy(1).wait_recv()
    absorb(0, 2)
    lax.fori_loop(1, block, absorb_pair, 0)
    for place in near_places(1)[1:]:
        take(place)
    lax.fori_loop(half // 2, half, embed, 0)

    keys_ids = []
    for i in range(half):
        place = sum(((i >> b) & 1) << (bits - 2 - b) for b in range(bits - 1))
        for p in (place, place + half):
            k = sum(((p >> b) & 1) << (bits - 1 - b) for b in range(bits))
            keys_ids.append(notes[k, per_owner : per_owner + 1])
    keys_ids = jnp.concatenate(keys_ids, axis=1).astype(jnp.float32)
    own_ids = jnp.transpose(
        jnp.broadcast_to(window_ids.astype(jnp.float32), (src_rows, src_rows))
    )[:, 0:1]
    same = own_ids == keys_ids
    same = jnp.concatenate([same, same], axis=0)
    columns = lax.broadcasted_iota(jnp.int32, (src_rows, inner), 1)

    def window_heads(pair, _):
        insides = [
            (columns >= h * VHD) & (columns < (h + 1) * VHD) for h in (2 * pair, 2 * pair + 1)
        ]
        wide = own_query[...].astype(jnp.float32)
        stacked = jnp.concatenate(
            [jnp.where(inside, wide, 0.0) for inside in insides], axis=0
        ).astype(jnp.bfloat16)
        scores = lax.dot_general(
            stacked, vision_kv[:, 0:inner], contract, preferred_element_type=jnp.float32
        ) * VHD ** (-0.5)
        scores = jnp.where(same, scores, DEAD)
        weights = jnp.exp(scores - jnp.max(scores, axis=1, keepdims=True))
        totals = jnp.sum(weights, axis=1, keepdims=True)
        blended = (
            jnp.dot(
                weights.astype(jnp.bfloat16), vision_kv[:, inner:], preferred_element_type=jnp.float32
            )
            / totals
        )
        held = pieces[...]
        held = jnp.where(insides[0], blended[0:src_rows], held)
        pieces[...] = jnp.where(insides[1], blended[src_rows:], held)
        return 0

    pieces[...] = jnp.zeros_like(pieces)
    lax.fori_loop(0, VHEADS // 2, window_heads, 0)
    vision_ref[...] = pieces[...].astype(jnp.bfloat16)
    lax.fori_loop(block, half - 1, absorb_pair, 0)
    last = pair_at(half - 1)
    for k in (last, last + 1):
        span_copy(k).wait_recv()
        absorb(k, 1)
    for h in range(QHEADS):
        rows = slice(h * tokens, (h + 1) * tokens)
        span_ref[:, h * HD : (h + 1) * HD] = (
            blend[rows] / jnp.sum(total[rows], axis=1, keepdims=True)
        ).astype(jnp.bfloat16)
    for k in others:
        patch_copy(k).wait_send()
        span_copy(k).wait_send()


def routed(
    devices, patches, row_owner, window_slot, w_patch, vit_gain, w_qkv, queries, new_kv,
    kv_cache, block_table,
):
    src_rows, patch = patches.shape
    vit = w_patch.shape[1]
    inner = VHEADS * VHD
    tokens, width = new_kv.shape
    blocks_dev, block_tokens, _ = kv_cache.shape
    per_owner = 2 * block_table.shape[1] // devices
    keys = devices * per_owner * block_tokens
    rows = QHEADS * tokens
    bf16, f32 = jnp.bfloat16, jnp.float32
    vmem, anywhere = pl.BlockSpec(memory_space=pltpu.VMEM), pl.BlockSpec(memory_space=pl.ANY)
    dma = pltpu.SemaphoreType.DMA
    return pl.pallas_call(
        functools.partial(route_kernel, devices, (vit, blocks_dev, block_tokens, per_owner)),
        out_shape=(
            jax.ShapeDtypeStruct((src_rows, inner), bf16),
            jax.ShapeDtypeStruct(queries.shape, bf16),
        ),
        in_specs=[
            anywhere, vmem, vmem, anywhere, vmem, anywhere, anywhere, anywhere, anywhere, vmem,
        ],
        out_specs=(vmem, vmem),
        scratch_shapes=[
            pltpu.VMEM((devices, patch, src_rows), bf16),
            pltpu.VMEM((patch, vit), bf16),
            pltpu.VMEM((vit, 3 * inner), bf16),
            pltpu.VMEM(kv_cache.shape, bf16),
            pltpu.VMEM((rows, HD), bf16),
            pltpu.VMEM((tokens, width), bf16),
            pltpu.VMEM((devices, 2 * per_owner, HD), jnp.int32),
            pltpu.VMEM((devices * per_owner, HD), jnp.int32),
            pltpu.SMEM((devices * per_owner, HD), jnp.int32),
            pltpu.VMEM((keys, width), bf16),
            pltpu.VMEM((keys, width), bf16),
            pltpu.VMEM((devices, per_owner, HD), f32),
            pltpu.VMEM((src_rows, inner), bf16),
            pltpu.VMEM((devices * src_rows, 2 * inner), bf16),
            pltpu.VMEM((src_rows, inner), f32),
            pltpu.VMEM((rows, HD), f32),
            pltpu.VMEM((rows, HD), f32),
            pltpu.VMEM((rows, HD), f32),
            dma((5,)),
            dma((QHEADS,)),
            dma,
        ]
        + [dma((devices,))] * 6,
        compiler_params=pltpu.CompilerParams(
            collective_id=0, has_side_effects=True, vmem_limit_bytes=58 << 20
        ),
        name="route",
    )(
        patches.T, row_owner.reshape(1, src_rows), window_slot.reshape(1, src_rows), w_patch,
        vit_gain, w_qkv, queries, new_kv, kv_cache, block_table,
    )


def shards(
    patches,
    row_owner,
    window_slot,
    w_patch,
    vit_gain,
    w_qkv,
    queries,
    new_kv,
    kv_cache,
    block_table,
):
    devices = lax.axis_size("seq")
    per_owner = 2 * block_table.shape[1] // devices
    whole_tiles = patches.shape[0] == HD and per_owner == 8 and per_owner * kv_cache.shape[1] == HD
    powers = devices >= 16 and devices & (devices - 1) == 0
    if whole_tiles and powers and new_kv.shape[0] == HD and block_table.shape[1] < HD:
        return routed(
            devices, patches, row_owner, window_slot, w_patch, vit_gain, w_qkv, queries,
            new_kv, kv_cache, block_table,
        )
    table_row = block_table[0]
    table_len = table_row.shape[0]
    blocks_dev = kv_cache.shape[0]
    per_owner = max(1, 2 * table_len // devices)
    is_live = table_row >= 0
    holder = jnp.where(is_live, table_row // blocks_dev, -1)
    local_block = jnp.where(is_live, table_row % blocks_dev, 0)
    before_entry = jnp.arange(table_len)[:, None] > jnp.arange(table_len)[None, :]
    same_holder = (holder[:, None] == holder[None, :]) & is_live[None, :] & before_entry
    holder_rank = jnp.sum(same_holder.astype(jnp.int32), axis=1)
    request_slot = jnp.where(is_live, holder * per_owner + holder_rank, devices * per_owner)
    slot_hits = request_slot[:, None] == jnp.arange(devices * per_owner)[None, :]
    wanted = jnp.sum(jnp.where(slot_hits, local_block[:, None], 0), axis=0).astype(jnp.int32)
    asked = lax.all_to_all(
        wanted.reshape(devices, per_owner), "seq", split_axis=0, concat_axis=0, tiled=True
    )
    fetched = kv_cache[asked]
    delivered = lax.all_to_all(fetched, "seq", split_axis=0, concat_axis=0, tiled=True)

    src_rows = patches.shape[0]
    capacity = max(1, 2 * src_rows // devices)
    slot_count = devices * capacity
    owner_ids = row_owner[:, 0]
    owner_hits = (owner_ids[:, None] == jnp.arange(devices)[None, :]).astype(jnp.bfloat16)
    strictly_lower = (jnp.arange(src_rows)[:, None] > jnp.arange(src_rows)[None, :]).astype(
        jnp.bfloat16
    )
    earlier = jnp.dot(strictly_lower, owner_hits, preferred_element_type=jnp.float32)
    ranks = jnp.sum(earlier * owner_hits.astype(jnp.float32), axis=1).astype(jnp.int32)
    target_slot = owner_ids * capacity + ranks
    row_hits = jnp.arange(slot_count)[:, None] == target_slot[None, :]
    window_buffer = jnp.sum(jnp.where(row_hits, window_slot[None, :] + 1, 0), axis=1) - 1
    normed = embed_rows(patches, w_patch, vit_gain)
    outgoing = jnp.dot(
        row_hits.astype(jnp.bfloat16), normed, preferred_element_type=jnp.float32
    ).astype(jnp.bfloat16)
    tag = jnp.broadcast_to(window_buffer.astype(jnp.bfloat16)[:, None], (slot_count, HD))
    outgoing, fetched = lax.optimization_barrier(
        (jnp.concatenate([outgoing, tag], axis=1), fetched)
    )
    arrived = lax.all_to_all(
        outgoing.reshape(devices, capacity, -1), "seq", split_axis=0, concat_axis=0, tiled=True
    ).reshape(slot_count, -1)
    vit = normed.shape[1]
    arrived_windows = arrived[:, vit].astype(jnp.int32)
    qkv_rows = jnp.dot(arrived[:, :vit], w_qkv, preferred_element_type=jnp.float32).astype(
        jnp.bfloat16
    )
    attended = window_attention(qkv_rows, arrived_windows)
    returned = lax.all_to_all(
        attended.reshape(devices, capacity, -1), "seq", split_axis=0, concat_axis=0, tiled=True
    )
    vision_out = jnp.dot(
        row_hits.T.astype(jnp.bfloat16),
        returned.reshape(slot_count, -1),
        preferred_element_type=jnp.float32,
    ).astype(jnp.bfloat16)
    slots = jnp.where(is_live, request_slot, 0).astype(jnp.int32)
    attention_out = prompt_attention(
        queries,
        new_kv,
        delivered.reshape((devices * per_owner,) + kv_cache.shape[1:]),
        slots,
        is_live,
    )
    return (vision_out, attention_out)


def solution(mesh):
    in_specs = (
        P(("groups", "seq"), None),
        P(("groups", "seq"), None),
        P(("groups", "seq")),
        P(),
        P(),
        P(),
        P(("groups", "seq"), None),
        P(("groups", "seq"), None),
        P(("groups", "seq"), None, None),
        P(("groups", "seq"), None),
    )
    out_specs = (P(("groups", "seq"), None), P(("groups", "seq"), None))
    return jax.shard_map(shards, mesh=mesh, in_specs=in_specs, out_specs=out_specs, check_vma=False)
```

```python
import functools

import jax
import jax.numpy as jnp
from jax import lax
from jax.experimental import pallas as pl
from jax.experimental.pallas import tpu as pltpu
from jax.sharding import PartitionSpec as P

VHEADS = 8
VHD = 80
QHEADS = 32
KVH = 4
HD = 128
DEAD = -1e30
EARLY = (8, 9, 1)
MIDDLE = (12, 10, 13, 11)
LATE = (14, 15, 5, 4, 7, 6, 3, 2)
OUTER_ORDER = (0, 6, 1, 7, 4, 2, 3, 5)
INNER_ORDER = (0, 4, 1, 5, 2, 3, 6, 7)


def embed_rows(patch_rows, w_patch, vit_gain):
    embedded = jnp.dot(patch_rows, w_patch, preferred_element_type=jnp.float32).astype(jnp.bfloat16)
    widened = lax.optimization_barrier(embedded).astype(jnp.float32)
    factor = lax.rsqrt(jnp.mean(widened * widened, axis=1, keepdims=True) + 1e-06)
    return (widened * factor * vit_gain).astype(jnp.bfloat16)


def window_attention(qkv_rows, windows):
    total_rows = qkv_rows.shape[0]
    inner_width = VHEADS * VHD
    query_heads = qkv_rows[:, :inner_width].reshape(total_rows, VHEADS, VHD)
    key_heads = qkv_rows[:, inner_width : 2 * inner_width].reshape(total_rows, VHEADS, VHD)
    value_heads = qkv_rows[:, 2 * inner_width :].reshape(total_rows, VHEADS, VHD)
    is_live = windows >= 0
    every_row = jnp.arange(total_rows)
    scores = jnp.einsum(
        "qhd,khd->hqk", query_heads, key_heads, preferred_element_type=jnp.float32
    ) * VHD ** (-0.5)
    allowed = (windows[:, None] == windows[None, :]) & is_live[None, :] | (
        every_row[:, None] == every_row[None, :]
    )
    scores = jnp.where(allowed[None], scores, -jnp.inf)
    highest = jnp.max(scores, axis=2, keepdims=True)
    weights = jnp.exp(scores - highest)
    totals = jnp.sum(weights, axis=2)
    blended = jnp.einsum(
        "hqk,khd->qhd",
        weights.astype(jnp.bfloat16),
        value_heads,
        preferred_element_type=jnp.float32,
    )
    pieces = (blended / totals.T[:, :, None]).reshape(total_rows, inner_width)
    return pieces.astype(jnp.bfloat16)


def span_kernel(slots, q_ref, fresh_ref, bias_ref, kv_ref, o_ref, held, sems):
    tokens = q_ref.shape[0]
    table_len, block_tokens = held.shape[0] - tokens // kv_ref.shape[1], kv_ref.shape[1]
    group_size = QHEADS // KVH
    width = held.shape[2]

    def copy_of(t):
        return pltpu.make_async_copy(kv_ref.at[slots[t]], held.at[t], sems.at[t])

    fresh_copy = pltpu.make_async_copy(
        fresh_ref, held.at[pl.ds(table_len, tokens // block_tokens)], sems.at[table_len]
    )
    fresh_copy.start()
    for t in range(table_len):
        copy_of(t).start()
    for t in range(table_len):
        copy_of(t).wait()
    fresh_copy.wait()
    keys = held.shape[0] * block_tokens
    rows = 2 * tokens
    causal = lax.broadcasted_iota(jnp.int32, (rows, keys), 1) - table_len * block_tokens <= lax.rem(
        lax.broadcasted_iota(jnp.int32, (rows, keys), 0), tokens
    )
    bias = jnp.where(causal, bias_ref[...], DEAD)
    for g in range(KVH):
        key_head = held[:, :, g * HD : (g + 1) * HD].reshape(keys, HD)
        value_head = held[:, :, width // 2 + g * HD : width // 2 + (g + 1) * HD].reshape(keys, HD)
        for pair in range(group_size // 2):
            first = g * group_size + 2 * pair
            query = jnp.concatenate(
                [q_ref[:, (first + i) * HD : (first + i + 1) * HD] for i in range(2)], axis=0
            )
            scores = lax.dot_general(
                query, key_head, (((1,), (1,)), ((), ())), preferred_element_type=jnp.float32
            ) * HD ** (-0.5) + bias
            highest = jnp.max(scores, axis=1, keepdims=True)
            weights = jnp.exp(scores - highest)
            totals = jnp.sum(weights, axis=1, keepdims=True)
            blended = jnp.dot(
                weights.astype(jnp.bfloat16), value_head, preferred_element_type=jnp.float32
            )
            out = (blended / totals).astype(jnp.bfloat16)
            for i in range(2):
                o_ref[:, (first + i) * HD : (first + i + 1) * HD] = out[i * tokens : (i + 1) * tokens]


def prompt_attention(queries, new_kv, delivered, slots, table_live):
    tokens = queries.shape[0]
    table_len = slots.shape[0]
    block_tokens, width = delivered.shape[1:]
    held_blocks = table_len + tokens // block_tokens
    bias = jnp.concatenate(
        [
            jnp.where(jnp.repeat(table_live, block_tokens), 0.0, DEAD),
            jnp.zeros((tokens,), jnp.float32),
        ]
    ).astype(jnp.float32)[None, :]
    return pl.pallas_call(
        span_kernel,
        out_shape=jax.ShapeDtypeStruct(queries.shape, jnp.bfloat16),
        grid_spec=pltpu.PrefetchScalarGridSpec(
            num_scalar_prefetch=1,
            in_specs=[
                pl.BlockSpec(memory_space=pltpu.VMEM),
                pl.BlockSpec(memory_space=pl.ANY),
                pl.BlockSpec(memory_space=pltpu.VMEM),
                pl.BlockSpec(memory_space=pl.ANY),
            ],
            out_specs=pl.BlockSpec(memory_space=pltpu.VMEM),
            scratch_shapes=[
                pltpu.VMEM((held_blocks, block_tokens, width), jnp.bfloat16),
                pltpu.SemaphoreType.DMA((table_len + 1,)),
            ],
        ),
        compiler_params=pltpu.CompilerParams(vmem_limit_bytes=40 << 20),
        name="span",
    )(slots, queries, new_kv.reshape(tokens // block_tokens, block_tokens, width), bias, delivered)


def route_kernel(
    devices,
    scale_dims,
    patches_hbm,
    owner_ref,
    window_ref,
    w_patch_hbm,
    gain_ref,
    w_qkv_hbm,
    queries_hbm,
    fresh_hbm,
    cache_hbm,
    table_ref,
    vision_ref,
    span_ref,
    patches,
    w_patch,
    w_qkv,
    cache,
    query,
    fresh,
    notes,
    picks,
    picks_smem,
    staged,
    spans,
    span_bias,
    own_query,
    vision_kv,
    pieces,
    top,
    total,
    blend,
    load_sems,
    query_sems,
    pick_sem,
    note_send,
    note_recv,
    patch_send,
    patch_recv,
    span_send,
    span_recv,
):
    vit, blocks_dev, block_tokens, per_owner = scale_dims
    me = lax.axis_index("seq")
    tokens = fresh.shape[0]
    src_rows = owner_ref.shape[1]
    chunk = per_owner * block_tokens
    inner = VHEADS * VHD
    group_rows = QHEADS // KVH * tokens
    kv_width = KVH * HD
    half = devices // 2
    bits = devices.bit_length() - 1

    def peer(k):
        other = me
        bit = 1
        while bit < devices:
            other = other + bit * ((k // bit) % 2) * (1 - 2 * ((me // bit) % 2))
            bit *= 2
        return other

    def remote(src, dst, send, recv, i, k):
        return pltpu.make_async_remote_copy(
            src_ref=src,
            dst_ref=dst,
            send_sem=send.at[i],
            recv_sem=recv.at[i],
            device_id={"seq": peer(k)},
            device_id_type=pl.DeviceIdType.MESH,
        )

    def note_copy(k):
        return remote(notes.at[0], notes.at[k], note_send, note_recv, k, k)

    def patch_copy(place):
        step = place.bit_length() - 1
        return remote(
            patches.at[place - (1 << step)],
            patches.at[place],
            patch_send,
            patch_recv,
            place,
            devices >> (step + 1),
        )

    def forward(place):
        step = place.bit_length()
        while (1 << step) < devices:
            patch_copy(place + (1 << step)).start()
            step += 1

    def take(place):
        patch_copy(place).wait_recv()
        forward(place)

    def span_copy(k):
        base = k * chunk
        rows = pl.ds(base if isinstance(k, int) else pl.multiple_of(base, chunk), chunk)
        return remote(staged.at[rows], spans.at[rows], span_send, span_recv, k, k)

    others = range(1, devices)
    barrier = pltpu.get_barrier_semaphore()
    for k in others:
        pl.semaphore_signal(
            barrier, inc=1, device_id={"seq": peer(k)}, device_id_type=pl.DeviceIdType.MESH
        )
    pairs = (
        (patches_hbm, patches.at[0]),
        (cache_hbm, cache),
        (fresh_hbm, fresh),
        (w_patch_hbm, w_patch),
        (w_qkv_hbm, w_qkv),
    )
    loads = [pltpu.make_async_copy(a, b, load_sems.at[i]) for i, (a, b) in enumerate(pairs)]
    query_loads = [
        pltpu.make_async_copy(
            queries_hbm.at[:, pl.ds(h * HD, HD)],
            query.at[pl.ds(h * tokens, tokens)],
            query_sems.at[h],
        )
        for h in range(QHEADS)
    ]
    for load in loads[:2]:
        load.start()
    table = jnp.concatenate(
        [table_ref[...], jnp.full((1, HD - table_ref.shape[1]), -1, jnp.int32)], axis=1
    )
    window_ids = window_ref[...] * devices + owner_ref[...]
    notes[0] = jnp.concatenate([table, window_ids], axis=0)
    pl.semaphore_wait(barrier, devices - 1)
    for k in reversed(others):
        note_copy(k).start()
    loads[0].wait()
    forward(0)
    for load in loads[2:3] + query_loads + loads[3:]:
        load.start()

    for k in others:
        note_copy(k).wait()
    asked = jnp.concatenate(
        [jnp.broadcast_to(notes[k, 0:1], (per_owner, HD)) for k in range(devices)], axis=0
    )
    first = me * blocks_dev
    hits = (asked >= first) & (asked < first + blocks_dev)
    before = (
        lax.broadcasted_iota(jnp.int32, (HD, HD), 0) < lax.broadcasted_iota(jnp.int32, (HD, HD), 1)
    )
    places = jnp.dot(
        jnp.where(hits, 1.0, 0.0).astype(jnp.bfloat16),
        jnp.where(before, 1.0, 0.0).astype(jnp.bfloat16),
        preferred_element_type=jnp.float32,
    ).astype(jnp.int32)
    turn = lax.rem(lax.broadcasted_iota(jnp.int32, asked.shape, 0), per_owner)
    local = jnp.sum(
        jnp.where(hits & (places == turn), (asked - first).astype(jnp.float32), 0.0),
        axis=1,
        keepdims=True,
    ).astype(jnp.int32)
    picks[...] = jnp.broadcast_to(local, picks.shape)
    pick_copy = pltpu.make_async_copy(picks, picks_smem, pick_sem)
    pick_copy.start()
    loads[1].wait()
    pick_copy.wait()

    def gather(k):
        target = staged if k else spans
        for s in range(per_owner):
            pick = jnp.clip(picks_smem[k * per_owner + s, 0], 0, blocks_dev - 1)
            target[pl.ds(k * chunk + s * block_tokens, block_tokens), :] = cache[pick]

    for k in EARLY + (0,) + MIDDLE + LATE:
        gather(k)
    quarter = me // (devices // 4)
    outer = (quarter == 0) | (quarter == 3)

    for k in EARLY:
        span_copy(k).start()
    own = jnp.broadcast_to(table, (per_owner, HD))
    step = lax.broadcasted_iota(jnp.int32, (per_owner, HD), 1)
    for k in range(devices):
        first = peer(k) * blocks_dev
        mine = (own >= first) & (own < first + blocks_dev)
        count = jnp.sum(jnp.where(mine, 1.0, 0.0), axis=1, keepdims=True).astype(jnp.int32)
        span_bias[k] = jnp.where(step < count * block_tokens, 0.0, DEAD)

    flip = (((0,), (0,)), ((), ()))
    contract = (((1,), (1,)), ((), ()))
    loads[2].wait()
    for load in query_loads:
        load.wait()
    causal = lax.rem(
        lax.broadcasted_iota(jnp.int32, (group_rows, tokens), 0), tokens
    ) >= lax.broadcasted_iota(jnp.int32, (group_rows, tokens), 1)
    for g in range(KVH):
        rows = slice(g * group_rows, (g + 1) * group_rows)
        scores = lax.dot_general(
            query[rows], fresh[:, g * HD : (g + 1) * HD], contract, preferred_element_type=jnp.float32
        ) * HD ** (-0.5)
        scores = jnp.where(causal, scores, DEAD)
        highest = jnp.max(scores, axis=1, keepdims=True)
        weights = jnp.exp(scores - highest)
        top[rows] = jnp.broadcast_to(highest, (group_rows, HD))
        total[rows] = weights
        blend[rows] = jnp.dot(
            weights.astype(jnp.bfloat16),
            fresh[:, kv_width + g * HD : kv_width + (g + 1) * HD],
            preferred_element_type=jnp.float32,
        )

    def near_places(offset):
        return [p for p in range(devices) if p % 2 == offset]

    @pl.when(jnp.logical_not(outer))
    def _():
        take(1)

    for place in near_places(0)[1:]:
        take(place)

    @pl.when(outer)
    def _():
        take(1)

    for k in MIDDLE:
        span_copy(k).start()

    def embed(i, _):
        place = 0
        for b in range(bits - 1):
            place = place + ((i // (1 << b)) % 2) * (1 << (bits - 2 - b))
        rows = jnp.concatenate([patches[place], patches[place + half]], axis=1)
        embedded = (
            lax.dot_general(rows, w_patch[...], flip, preferred_element_type=jnp.float32)
            .astype(jnp.bfloat16)
            .astype(jnp.float32)
        )
        factor = lax.rsqrt(jnp.mean(embedded * embedded, axis=1, keepdims=True) + 1e-06)
        normed = (embedded * factor * gain_ref[...].reshape(1, vit)).astype(jnp.bfloat16)
        vision_kv[pl.ds(pl.multiple_of(i * 2 * src_rows, 2 * src_rows), 2 * src_rows), :] = jnp.dot(
            normed, w_qkv[:, inner:], preferred_element_type=jnp.float32
        ).astype(jnp.bfloat16)

        @pl.when(i == 0)
        def _():
            own_query[...] = jnp.dot(
                normed[0:src_rows], w_qkv[:, 0:inner], preferred_element_type=jnp.float32
            ).astype(jnp.bfloat16)

        return 0

    def absorb(k, width):
        base = k * chunk
        bias = jnp.concatenate([span_bias[k + i, 0:1] for i in range(width)], axis=1)
        span = pl.ds(pl.multiple_of(base, chunk), width * chunk)
        for g in range(KVH):
            rows = slice(g * group_rows, (g + 1) * group_rows)
            scores = lax.dot_general(
                query[rows],
                spans[span, g * HD : (g + 1) * HD],
                contract,
                preferred_element_type=jnp.float32,
            ) * HD ** (-0.5) + bias
            old = top[rows]
            highest = jnp.maximum(old, jnp.max(scores, axis=1, keepdims=True))
            shrink = jnp.exp(old - highest)
            parts = [
                jnp.exp(scores[:, i * chunk : (i + 1) * chunk] - highest) for i in range(width)
            ]
            summed = total[rows] * shrink
            for part in parts:
                summed = summed + part
            weights = jnp.concatenate([part.astype(jnp.bfloat16) for part in parts], axis=1)
            top[rows] = highest
            total[rows] = summed
            blend[rows] = blend[rows] * shrink + jnp.dot(
                weights,
                spans[span, kv_width + g * HD : kv_width + (g + 1) * HD],
                preferred_element_type=jnp.float32,
            )

    def pair_at(j):
        pair = 0
        for i, (a, b) in enumerate(zip(OUTER_ORDER, INNER_ORDER)):
            pair = jnp.where(j == i, jnp.where(outer, a, b), pair)
        return 2 * pair

    def absorb_pair(j, _):
        k = pair_at(j)
        span_copy(k).wait_recv()
        span_copy(k + 1).wait_recv()
        absorb(k, 2)
        return 0

    loads[3].wait()
    loads[4].wait()
    lax.fori_loop(0, half // 2, embed, 0)
    take(3)
    for k in LATE:
        span_copy(k).start()
    span_copy(1).wait_recv()
    absorb(0, 2)
    take(5)
    lax.fori_loop(1, 2, absorb_pair, 0)
    take(7)
    for place in near_places(1)[4:]:
        take(place)
    lax.fori_loop(half // 2, half, embed, 0)

    keys_ids = []
    for i in range(half):
        place = sum(((i >> b) & 1) << (bits - 2 - b) for b in range(bits - 1))
        for p in (place, place + half):
            k = sum(((p >> b) & 1) << (bits - 1 - b) for b in range(bits))
            keys_ids.append(notes[k, 1:2])
    keys_ids = jnp.concatenate(keys_ids, axis=1).astype(jnp.float32)
    own_ids = jnp.transpose(
        jnp.broadcast_to(window_ids.astype(jnp.float32), (src_rows, src_rows))
    )[:, 0:1]
    same = own_ids == keys_ids
    same = jnp.concatenate([same, same], axis=0)
    columns = lax.broadcasted_iota(jnp.int32, (src_rows, inner), 1)

    def window_heads(pair, _):
        insides = [
            (columns >= h * VHD) & (columns < (h + 1) * VHD) for h in (2 * pair, 2 * pair + 1)
        ]
        wide = own_query[...].astype(jnp.float32)
        stacked = jnp.concatenate(
            [jnp.where(inside, wide, 0.0) for inside in insides], axis=0
        ).astype(jnp.bfloat16)
        scores = lax.dot_general(
            stacked, vision_kv[:, 0:inner], contract, preferred_element_type=jnp.float32
        ) * VHD ** (-0.5)
        scores = jnp.where(same, scores, DEAD)
        weights = jnp.exp(scores - jnp.max(scores, axis=1, keepdims=True))
        totals = jnp.sum(weights, axis=1, keepdims=True)
        blended = (
            jnp.dot(
                weights.astype(jnp.bfloat16), vision_kv[:, inner:], preferred_element_type=jnp.float32
            )
            / totals
        )
        held = pieces[...]
        held = jnp.where(insides[0], blended[0:src_rows], held)
        pieces[...] = jnp.where(insides[1], blended[src_rows:], held)
        return 0

    pieces[...] = jnp.zeros_like(pieces)
    lax.fori_loop(0, VHEADS // 2, window_heads, 0)
    vision_ref[...] = pieces[...].astype(jnp.bfloat16)
    lax.fori_loop(2, half - 1, absorb_pair, 0)
    last = pair_at(half - 1)
    for k in (last, last + 1):
        span_copy(k).wait_recv()
        absorb(k, 1)
    for h in range(QHEADS):
        rows = slice(h * tokens, (h + 1) * tokens)
        span_ref[:, h * HD : (h + 1) * HD] = (
            blend[rows] / jnp.sum(total[rows], axis=1, keepdims=True)
        ).astype(jnp.bfloat16)
    for k in others:
        patch_copy(k).wait_send()
        span_copy(k).wait_send()


def routed(
    devices, patches, row_owner, window_slot, w_patch, vit_gain, w_qkv, queries, new_kv,
    kv_cache, block_table,
):
    src_rows, patch = patches.shape
    vit = w_patch.shape[1]
    inner = VHEADS * VHD
    tokens, width = new_kv.shape
    blocks_dev, block_tokens, _ = kv_cache.shape
    per_owner = 2 * block_table.shape[1] // devices
    keys = devices * per_owner * block_tokens
    rows = QHEADS * tokens
    bf16, f32 = jnp.bfloat16, jnp.float32
    vmem, anywhere = pl.BlockSpec(memory_space=pltpu.VMEM), pl.BlockSpec(memory_space=pl.ANY)
    dma = pltpu.SemaphoreType.DMA
    return pl.pallas_call(
        functools.partial(route_kernel, devices, (vit, blocks_dev, block_tokens, per_owner)),
        out_shape=(
            jax.ShapeDtypeStruct((src_rows, inner), bf16),
            jax.ShapeDtypeStruct(queries.shape, bf16),
        ),
        in_specs=[
            anywhere, vmem, vmem, anywhere, vmem, anywhere, anywhere, anywhere, anywhere, vmem,
        ],
        out_specs=(vmem, vmem),
        scratch_shapes=[
            pltpu.VMEM((devices, patch, src_rows), bf16),
            pltpu.VMEM((patch, vit), bf16),
            pltpu.VMEM((vit, 3 * inner), bf16),
            pltpu.VMEM(kv_cache.shape, bf16),
            pltpu.VMEM((rows, HD), bf16),
            pltpu.VMEM((tokens, width), bf16),
            pltpu.VMEM((devices, 2, HD), jnp.int32),
            pltpu.VMEM((devices * per_owner, HD), jnp.int32),
            pltpu.SMEM((devices * per_owner, HD), jnp.int32),
            pltpu.VMEM((keys, width), bf16),
            pltpu.VMEM((keys, width), bf16),
            pltpu.VMEM((devices, per_owner, HD), f32),
            pltpu.VMEM((src_rows, inner), bf16),
            pltpu.VMEM((devices * src_rows, 2 * inner), bf16),
            pltpu.VMEM((src_rows, inner), f32),
            pltpu.VMEM((rows, HD), f32),
            pltpu.VMEM((rows, HD), f32),
            pltpu.VMEM((rows, HD), f32),
            dma((5,)),
            dma((QHEADS,)),
            dma,
        ]
        + [dma((devices,))] * 6,
        compiler_params=pltpu.CompilerParams(
            collective_id=0, has_side_effects=True, vmem_limit_bytes=58 << 20
        ),
        name="route",
    )(
        patches.T, row_owner.reshape(1, src_rows), window_slot.reshape(1, src_rows), w_patch,
        vit_gain, w_qkv, queries, new_kv, kv_cache, block_table,
    )


def shards(
    patches,
    row_owner,
    window_slot,
    w_patch,
    vit_gain,
    w_qkv,
    queries,
    new_kv,
    kv_cache,
    block_table,
):
    devices = lax.axis_size("seq")
    per_owner = 2 * block_table.shape[1] // devices
    whole_tiles = patches.shape[0] == HD and per_owner == 8 and per_owner * kv_cache.shape[1] == HD
    ordered = devices == 1 + len(EARLY + MIDDLE + LATE)
    if whole_tiles and ordered and new_kv.shape[0] == HD and block_table.shape[1] < HD:
        return routed(
            devices, patches, row_owner, window_slot, w_patch, vit_gain, w_qkv, queries,
            new_kv, kv_cache, block_table,
        )
    table_row = block_table[0]
    table_len = table_row.shape[0]
    blocks_dev = kv_cache.shape[0]
    per_owner = max(1, 2 * table_len // devices)
    is_live = table_row >= 0
    holder = jnp.where(is_live, table_row // blocks_dev, -1)
    local_block = jnp.where(is_live, table_row % blocks_dev, 0)
    before_entry = jnp.arange(table_len)[:, None] > jnp.arange(table_len)[None, :]
    same_holder = (holder[:, None] == holder[None, :]) & is_live[None, :] & before_entry
    holder_rank = jnp.sum(same_holder.astype(jnp.int32), axis=1)
    request_slot = jnp.where(is_live, holder * per_owner + holder_rank, devices * per_owner)
    slot_hits = request_slot[:, None] == jnp.arange(devices * per_owner)[None, :]
    wanted = jnp.sum(jnp.where(slot_hits, local_block[:, None], 0), axis=0).astype(jnp.int32)
    asked = lax.all_to_all(
        wanted.reshape(devices, per_owner), "seq", split_axis=0, concat_axis=0, tiled=True
    )
    fetched = kv_cache[asked]
    delivered = lax.all_to_all(fetched, "seq", split_axis=0, concat_axis=0, tiled=True)

    src_rows = patches.shape[0]
    capacity = max(1, 2 * src_rows // devices)
    slot_count = devices * capacity
    owner_ids = row_owner[:, 0]
    owner_hits = (owner_ids[:, None] == jnp.arange(devices)[None, :]).astype(jnp.bfloat16)
    strictly_lower = (jnp.arange(src_rows)[:, None] > jnp.arange(src_rows)[None, :]).astype(
        jnp.bfloat16
    )
    earlier = jnp.dot(strictly_lower, owner_hits, preferred_element_type=jnp.float32)
    ranks = jnp.sum(earlier * owner_hits.astype(jnp.float32), axis=1).astype(jnp.int32)
    target_slot = owner_ids * capacity + ranks
    row_hits = jnp.arange(slot_count)[:, None] == target_slot[None, :]
    window_buffer = jnp.sum(jnp.where(row_hits, window_slot[None, :] + 1, 0), axis=1) - 1
    normed = embed_rows(patches, w_patch, vit_gain)
    outgoing = jnp.dot(
        row_hits.astype(jnp.bfloat16), normed, preferred_element_type=jnp.float32
    ).astype(jnp.bfloat16)
    tag = jnp.broadcast_to(window_buffer.astype(jnp.bfloat16)[:, None], (slot_count, HD))
    outgoing, fetched = lax.optimization_barrier(
        (jnp.concatenate([outgoing, tag], axis=1), fetched)
    )
    arrived = lax.all_to_all(
        outgoing.reshape(devices, capacity, -1), "seq", split_axis=0, concat_axis=0, tiled=True
    ).reshape(slot_count, -1)
    vit = normed.shape[1]
    arrived_windows = arrived[:, vit].astype(jnp.int32)
    qkv_rows = jnp.dot(arrived[:, :vit], w_qkv, preferred_element_type=jnp.float32).astype(
        jnp.bfloat16
    )
    attended = window_attention(qkv_rows, arrived_windows)
    returned = lax.all_to_all(
        attended.reshape(devices, capacity, -1), "seq", split_axis=0, concat_axis=0, tiled=True
    )
    vision_out = jnp.dot(
        row_hits.T.astype(jnp.bfloat16),
        returned.reshape(slot_count, -1),
        preferred_element_type=jnp.float32,
    ).astype(jnp.bfloat16)
    slots = jnp.where(is_live, request_slot, 0).astype(jnp.int32)
    attention_out = prompt_attention(
        queries,
        new_kv,
        delivered.reshape((devices * per_owner,) + kv_cache.shape[1:]),
        slots,
        is_live,
    )
    return (vision_out, attention_out)


def solution(mesh):
    in_specs = (
        P(("groups", "seq"), None),
        P(("groups", "seq"), None),
        P(("groups", "seq")),
        P(),
        P(),
        P(),
        P(("groups", "seq"), None),
        P(("groups", "seq"), None),
        P(("groups", "seq"), None, None),
        P(("groups", "seq"), None),
    )
    out_specs = (P(("groups", "seq"), None), P(("groups", "seq"), None))
    return jax.shard_map(shards, mesh=mesh, in_specs=in_specs, out_specs=out_specs, check_vma=False)
```

```python
import functools

import jax
import jax.numpy as jnp
from jax import lax
from jax.experimental import pallas as pl
from jax.experimental.pallas import tpu as pltpu
from jax.sharding import PartitionSpec as P

VHEADS = 8
VHD = 80
QHEADS = 32
KVH = 4
PLACE_STEPS = 2
HD = 128
DEAD = -1e30
EARLY = (8, 9, 1)
MIDDLE = (12, 10, 13, 11)
LATE = (14, 15, 5, 4, 7, 6, 3, 2)
OUTER_ORDER = (0, 6, 1, 7, 4, 2, 3, 5)
INNER_ORDER = (0, 4, 1, 5, 2, 3, 6, 7)


def embed_rows(patch_rows, w_patch, vit_gain):
    embedded = jnp.dot(patch_rows, w_patch, preferred_element_type=jnp.float32).astype(jnp.bfloat16)
    widened = lax.optimization_barrier(embedded).astype(jnp.float32)
    factor = lax.rsqrt(jnp.mean(widened * widened, axis=1, keepdims=True) + 1e-06)
    return (widened * factor * vit_gain).astype(jnp.bfloat16)


def window_attention(qkv_rows, windows):
    total_rows = qkv_rows.shape[0]
    inner_width = VHEADS * VHD
    query_heads = qkv_rows[:, :inner_width].reshape(total_rows, VHEADS, VHD)
    key_heads = qkv_rows[:, inner_width : 2 * inner_width].reshape(total_rows, VHEADS, VHD)
    value_heads = qkv_rows[:, 2 * inner_width :].reshape(total_rows, VHEADS, VHD)
    is_live = windows >= 0
    every_row = jnp.arange(total_rows)
    scores = jnp.einsum(
        "qhd,khd->hqk", query_heads, key_heads, preferred_element_type=jnp.float32
    ) * VHD ** (-0.5)
    allowed = (windows[:, None] == windows[None, :]) & is_live[None, :] | (
        every_row[:, None] == every_row[None, :]
    )
    scores = jnp.where(allowed[None], scores, -jnp.inf)
    highest = jnp.max(scores, axis=2, keepdims=True)
    weights = jnp.exp(scores - highest)
    totals = jnp.sum(weights, axis=2)
    blended = jnp.einsum(
        "hqk,khd->qhd",
        weights.astype(jnp.bfloat16),
        value_heads,
        preferred_element_type=jnp.float32,
    )
    pieces = (blended / totals.T[:, :, None]).reshape(total_rows, inner_width)
    return pieces.astype(jnp.bfloat16)


def span_kernel(slots, q_ref, fresh_ref, bias_ref, kv_ref, o_ref, held, sems):
    tokens = q_ref.shape[0]
    table_len, block_tokens = held.shape[0] - tokens // kv_ref.shape[1], kv_ref.shape[1]
    group_size = QHEADS // KVH
    width = held.shape[2]

    def copy_of(t):
        return pltpu.make_async_copy(kv_ref.at[slots[t]], held.at[t], sems.at[t])

    fresh_copy = pltpu.make_async_copy(
        fresh_ref, held.at[pl.ds(table_len, tokens // block_tokens)], sems.at[table_len]
    )
    fresh_copy.start()
    for t in range(table_len):
        copy_of(t).start()
    for t in range(table_len):
        copy_of(t).wait()
    fresh_copy.wait()
    keys = held.shape[0] * block_tokens
    rows = 2 * tokens
    causal = lax.broadcasted_iota(jnp.int32, (rows, keys), 1) - table_len * block_tokens <= lax.rem(
        lax.broadcasted_iota(jnp.int32, (rows, keys), 0), tokens
    )
    bias = jnp.where(causal, bias_ref[...], DEAD)
    for g in range(KVH):
        key_head = held[:, :, g * HD : (g + 1) * HD].reshape(keys, HD)
        value_head = held[:, :, width // 2 + g * HD : width // 2 + (g + 1) * HD].reshape(keys, HD)
        for pair in range(group_size // 2):
            first = g * group_size + 2 * pair
            query = jnp.concatenate(
                [q_ref[:, (first + i) * HD : (first + i + 1) * HD] for i in range(2)], axis=0
            )
            scores = lax.dot_general(
                query, key_head, (((1,), (1,)), ((), ())), preferred_element_type=jnp.float32
            ) * HD ** (-0.5) + bias
            highest = jnp.max(scores, axis=1, keepdims=True)
            weights = jnp.exp(scores - highest)
            totals = jnp.sum(weights, axis=1, keepdims=True)
            blended = jnp.dot(
                weights.astype(jnp.bfloat16), value_head, preferred_element_type=jnp.float32
            )
            out = (blended / totals).astype(jnp.bfloat16)
            for i in range(2):
                o_ref[:, (first + i) * HD : (first + i + 1) * HD] = out[i * tokens : (i + 1) * tokens]


def prompt_attention(queries, new_kv, delivered, slots, table_live):
    tokens = queries.shape[0]
    table_len = slots.shape[0]
    block_tokens, width = delivered.shape[1:]
    held_blocks = table_len + tokens // block_tokens
    bias = jnp.concatenate(
        [
            jnp.where(jnp.repeat(table_live, block_tokens), 0.0, DEAD),
            jnp.zeros((tokens,), jnp.float32),
        ]
    ).astype(jnp.float32)[None, :]
    return pl.pallas_call(
        span_kernel,
        out_shape=jax.ShapeDtypeStruct(queries.shape, jnp.bfloat16),
        grid_spec=pltpu.PrefetchScalarGridSpec(
            num_scalar_prefetch=1,
            in_specs=[
                pl.BlockSpec(memory_space=pltpu.VMEM),
                pl.BlockSpec(memory_space=pl.ANY),
                pl.BlockSpec(memory_space=pltpu.VMEM),
                pl.BlockSpec(memory_space=pl.ANY),
            ],
            out_specs=pl.BlockSpec(memory_space=pltpu.VMEM),
            scratch_shapes=[
                pltpu.VMEM((held_blocks, block_tokens, width), jnp.bfloat16),
                pltpu.SemaphoreType.DMA((table_len + 1,)),
            ],
        ),
        compiler_params=pltpu.CompilerParams(vmem_limit_bytes=40 << 20),
        name="span",
    )(slots, queries, new_kv.reshape(tokens // block_tokens, block_tokens, width), bias, delivered)


def route_kernel(
    devices,
    scale_dims,
    patches_hbm,
    owner_hbm,
    window_hbm,
    w_patch_hbm,
    gain_hbm,
    w_qkv_hbm,
    queries_hbm,
    fresh_hbm,
    cache_hbm,
    table_hbm,
    vision_ref,
    span_ref,
    owner_ref,
    window_ref,
    gain_ref,
    table_ref,
    patches,
    w_patch,
    w_qkv,
    cache,
    query,
    fresh,
    notes,
    picks,
    picks_smem,
    staged,
    spans,
    span_bias,
    own_query,
    vision_kv,
    pieces,
    vision_rows,
    span_rows,
    top,
    total,
    blend,
    small_sems,
    load_sems,
    query_sems,
    pick_sem,
    note_send,
    note_recv,
    patch_send,
    patch_recv,
    span_send,
    span_recv,
    out_sems,
):
    vit, blocks_dev, block_tokens, per_owner = scale_dims
    me = lax.axis_index("seq")
    tokens = fresh.shape[0]
    src_rows = owner_ref.shape[1]
    chunk = per_owner * block_tokens
    inner = VHEADS * VHD
    group_rows = QHEADS // KVH * tokens
    kv_width = KVH * HD
    part = kv_width // 2
    half = devices // 2
    bits = devices.bit_length() - 1

    def peer(k):
        other = me
        bit = 1
        while bit < devices:
            other = other + bit * ((k // bit) % 2) * (1 - 2 * ((me // bit) % 2))
            bit *= 2
        return other

    def remote(src, dst, send, recv, i, k):
        return pltpu.make_async_remote_copy(
            src_ref=src,
            dst_ref=dst,
            send_sem=send.at[i],
            recv_sem=recv.at[i],
            device_id={"seq": peer(k)},
            device_id_type=pl.DeviceIdType.MESH,
        )

    def note_copy(k):
        return remote(notes.at[0], notes.at[k], note_send, note_recv, k, k)

    def patch_copy(place):
        step = place.bit_length() - 1
        return remote(
            patches.at[place - (1 << step)],
            patches.at[place],
            patch_send,
            patch_recv,
            place,
            devices >> (step + 1),
        )

    def forward(place):
        step = place.bit_length()
        while (1 << step) < devices:
            patch_copy(place + (1 << step)).start()
            step += 1

    def take(place):
        patch_copy(place).wait_recv()
        forward(place)

    def span_copy(k, side):
        base = k * chunk
        rows = pl.ds(base if isinstance(k, int) else pl.multiple_of(base, chunk), chunk)
        i = side * devices + k
        return remote(staged.at[side, rows], spans.at[side, rows], span_send, span_recv, i, k)

    def send_chunk(k):
        for side in range(2):
            span_copy(k, side).start()

    def take_chunk(k):
        for side in range(2):
            span_copy(k, side).wait_recv()

    others = range(1, devices)
    small = [
        pltpu.make_async_copy(a, b, small_sems.at[i])
        for i, (a, b) in enumerate(
            (
                (table_hbm, table_ref),
                (owner_hbm, owner_ref),
                (window_hbm, window_ref),
                (gain_hbm, gain_ref),
            )
        )
    ]
    for load in small:
        load.start()
    barrier = pltpu.get_barrier_semaphore()
    for k in others:
        pl.semaphore_signal(
            barrier, inc=1, device_id={"seq": peer(k)}, device_id_type=pl.DeviceIdType.MESH
        )
    pairs = (
        (patches_hbm, patches.at[0]),
        (cache_hbm, cache),
        (fresh_hbm, fresh),
        (w_patch_hbm, w_patch),
        (w_qkv_hbm, w_qkv),
    )
    loads = [pltpu.make_async_copy(a, b, load_sems.at[i]) for i, (a, b) in enumerate(pairs)]
    query_loads = [
        pltpu.make_async_copy(
            queries_hbm.at[:, pl.ds(h * HD, HD)],
            query.at[pl.ds(h * tokens, tokens)],
            query_sems.at[h],
        )
        for h in range(QHEADS)
    ]
    for load in loads[:2]:
        load.start()
    for load in small:
        load.wait()
    table = jnp.concatenate(
        [table_ref[...], jnp.full((1, HD - table_ref.shape[1]), -1, jnp.int32)], axis=1
    )
    window_ids = window_ref[...] * devices + owner_ref[...]
    notes[0] = jnp.concatenate([table, window_ids], axis=0)
    pl.semaphore_wait(barrier, devices - 1)
    for k in reversed(others):
        note_copy(k).start()
    loads[0].wait()
    forward(0)
    for load in loads[2:3] + query_loads + loads[3:]:
        load.start()

    for k in others:
        note_copy(k).wait()
    asked = jnp.concatenate(
        [jnp.broadcast_to(notes[k, 0:1], (per_owner, HD)) for k in range(devices)], axis=0
    )
    first = me * blocks_dev
    hits = (asked >= first) & (asked < first + blocks_dev)
    before = (
        lax.broadcasted_iota(jnp.int32, (HD, HD), 0) < lax.broadcasted_iota(jnp.int32, (HD, HD), 1)
    )
    places = jnp.dot(
        jnp.where(hits, 1.0, 0.0).astype(jnp.bfloat16),
        jnp.where(before, 1.0, 0.0).astype(jnp.bfloat16),
        preferred_element_type=jnp.float32,
    ).astype(jnp.int32)
    turn = lax.rem(lax.broadcasted_iota(jnp.int32, asked.shape, 0), per_owner)
    local = jnp.sum(
        jnp.where(hits & (places == turn), (asked - first).astype(jnp.float32), 0.0),
        axis=1,
        keepdims=True,
    ).astype(jnp.int32)
    picks[...] = jnp.broadcast_to(local, picks.shape)
    pick_copy = pltpu.make_async_copy(picks, picks_smem, pick_sem)
    pick_copy.start()
    loads[1].wait()
    pick_copy.wait()

    def gather(k):
        target = staged if k else spans
        for s in range(per_owner):
            pick = jnp.clip(picks_smem[k * per_owner + s, 0], 0, blocks_dev - 1)
            rows = pl.ds(k * chunk + s * block_tokens, block_tokens)
            block = cache[pick]
            for i in range(2):
                first = i * part
                target[i, rows, 0:part] = block[:, first : first + part]
                target[i, rows, part:] = block[:, kv_width + first : kv_width + first + part]

    for k in EARLY + (0,) + MIDDLE + LATE:
        gather(k)
    quarter = me // (devices // 4)
    outer = (quarter == 0) | (quarter == 3)

    for k in EARLY:
        send_chunk(k)
    own = jnp.broadcast_to(table, (per_owner, HD))
    step = lax.broadcasted_iota(jnp.int32, (per_owner, HD), 1)
    for k in range(devices):
        first = peer(k) * blocks_dev
        mine = (own >= first) & (own < first + blocks_dev)
        count = jnp.sum(jnp.where(mine, 1.0, 0.0), axis=1, keepdims=True).astype(jnp.int32)
        span_bias[k] = jnp.where(step < count * block_tokens, 0.0, DEAD)

    flip = (((0,), (0,)), ((), ()))
    contract = (((1,), (1,)), ((), ()))
    loads[2].wait()
    for load in query_loads:
        load.wait()
    causal = lax.rem(
        lax.broadcasted_iota(jnp.int32, (group_rows, tokens), 0), tokens
    ) >= lax.broadcasted_iota(jnp.int32, (group_rows, tokens), 1)
    for g in range(KVH):
        rows = slice(g * group_rows, (g + 1) * group_rows)
        scores = lax.dot_general(
            query[rows], fresh[:, g * HD : (g + 1) * HD], contract, preferred_element_type=jnp.float32
        ) * HD ** (-0.5)
        scores = jnp.where(causal, scores, DEAD)
        highest = jnp.max(scores, axis=1, keepdims=True)
        weights = jnp.exp(scores - highest)
        top[rows] = jnp.broadcast_to(highest, (group_rows, HD))
        total[rows] = weights
        blend[rows] = jnp.dot(
            weights.astype(jnp.bfloat16),
            fresh[:, kv_width + g * HD : kv_width + (g + 1) * HD],
            preferred_element_type=jnp.float32,
        )

    def near_places(offset):
        return [p for p in range(devices) if p % 2 == offset]

    @pl.when(jnp.logical_not(outer))
    def _():
        take(1)

    for place in near_places(0)[1:]:
        take(place)

    @pl.when(outer)
    def _():
        take(1)

    for k in MIDDLE:
        send_chunk(k)

    def embed(i, _):
        place = 0
        for b in range(bits - 1):
            place = place + ((i // (1 << b)) % 2) * (1 << (bits - 2 - b))
        rows = jnp.concatenate([patches[place], patches[place + half]], axis=1)
        embedded = (
            lax.dot_general(rows, w_patch[...], flip, preferred_element_type=jnp.float32)
            .astype(jnp.bfloat16)
            .astype(jnp.float32)
        )
        factor = lax.rsqrt(jnp.mean(embedded * embedded, axis=1, keepdims=True) + 1e-06)
        normed = (embedded * factor * gain_ref[...].reshape(1, vit)).astype(jnp.bfloat16)
        vision_kv[pl.ds(pl.multiple_of(i * 2 * src_rows, 2 * src_rows), 2 * src_rows), :] = jnp.dot(
            normed, w_qkv[:, inner:], preferred_element_type=jnp.float32
        ).astype(jnp.bfloat16)

        @pl.when(i == 0)
        def _():
            own_query[...] = jnp.dot(
                normed[0:src_rows], w_qkv[:, 0:inner], preferred_element_type=jnp.float32
            ).astype(jnp.bfloat16)

        return 0

    def merged(k, width, g):
        base = k * chunk
        bias = jnp.concatenate([span_bias[k + i, 0:1] for i in range(width)], axis=1)
        span = pl.ds(pl.multiple_of(base, chunk), width * chunk)
        side, column = g // (KVH // 2), g % (KVH // 2) * HD
        rows = slice(g * group_rows, (g + 1) * group_rows)
        scores = lax.dot_general(
            query[rows],
            spans[side, span, column : column + HD],
            contract,
            preferred_element_type=jnp.float32,
        ) * HD ** (-0.5) + bias
        old = top[rows]
        highest = jnp.maximum(old, jnp.max(scores, axis=1, keepdims=True))
        shrink = jnp.exp(old - highest)
        parts = [jnp.exp(scores[:, i * chunk : (i + 1) * chunk] - highest) for i in range(width)]
        summed = total[rows] * shrink
        for piece in parts:
            summed = summed + piece
        weights = jnp.concatenate([piece.astype(jnp.bfloat16) for piece in parts], axis=1)
        blended = blend[rows] * shrink + jnp.dot(
            weights,
            spans[side, span, part + column : part + column + HD],
            preferred_element_type=jnp.float32,
        )
        return highest, summed, blended

    def absorb(k, width):
        for g in range(KVH):
            rows = slice(g * group_rows, (g + 1) * group_rows)
            top[rows], total[rows], blend[rows] = merged(k, width, g)

    def pair_at(j):
        pair = 0
        for i, (a, b) in enumerate(zip(OUTER_ORDER, INNER_ORDER)):
            pair = jnp.where(j == i, jnp.where(outer, a, b), pair)
        return 2 * pair

    def absorb_pair(j, _):
        k = pair_at(j)
        take_chunk(k)
        take_chunk(k + 1)
        absorb(k, 2)
        return 0

    loads[3].wait()
    loads[4].wait()
    lax.fori_loop(0, half // 2, embed, 0)
    take(3)
    for k in LATE:
        send_chunk(k)
    take_chunk(1)
    absorb(0, 2)
    take(5)
    lax.fori_loop(1, 2, absorb_pair, 0)
    take(7)
    for place in near_places(1)[4:]:
        take(place)
    lax.fori_loop(half // 2, half, embed, 0)

    keys_ids = []
    for i in range(half):
        place = sum(((i >> b) & 1) << (bits - 2 - b) for b in range(bits - 1))
        for p in (place, place + half):
            k = sum(((p >> b) & 1) << (bits - 1 - b) for b in range(bits))
            keys_ids.append(notes[k, 1:2])
    keys_ids = jnp.concatenate(keys_ids, axis=1).astype(jnp.float32)
    own_ids = jnp.transpose(
        jnp.broadcast_to(window_ids.astype(jnp.float32), (src_rows, src_rows))
    )[:, 0:1]
    same = own_ids == keys_ids
    same = jnp.concatenate([same, same], axis=0)
    columns = lax.broadcasted_iota(jnp.int32, (src_rows, inner), 1)

    def window_heads(pair, _):
        insides = [
            (columns >= h * VHD) & (columns < (h + 1) * VHD) for h in (2 * pair, 2 * pair + 1)
        ]
        wide = own_query[...].astype(jnp.float32)
        stacked = jnp.concatenate(
            [jnp.where(inside, wide, 0.0) for inside in insides], axis=0
        ).astype(jnp.bfloat16)
        scores = lax.dot_general(
            stacked, vision_kv[:, 0:inner], contract, preferred_element_type=jnp.float32
        ) * VHD ** (-0.5)
        scores = jnp.where(same, scores, DEAD)
        weights = jnp.exp(scores - jnp.max(scores, axis=1, keepdims=True))
        totals = jnp.sum(weights, axis=1, keepdims=True)
        blended = (
            jnp.dot(
                weights.astype(jnp.bfloat16), vision_kv[:, inner:], preferred_element_type=jnp.float32
            )
            / totals
        )
        held = pieces[...]
        held = jnp.where(insides[0], blended[0:src_rows], held)
        pieces[...] = jnp.where(insides[1], blended[src_rows:], held)
        return 0

    pieces[...] = jnp.zeros_like(pieces)
    lax.fori_loop(0, VHEADS // 2, window_heads, 0)
    vision_rows[...] = pieces[...].astype(jnp.bfloat16)
    vision_write = pltpu.make_async_copy(vision_rows, vision_ref, out_sems.at[0])
    vision_write.start()
    lax.fori_loop(2, half - 1, absorb_pair, 0)
    last = pair_at(half - 1)
    take_chunk(last)
    absorb(last, 1)
    heads = QHEADS // KVH
    writes = [vision_write]
    for g in range(KVH):
        if g % (KVH // 2) == 0:
            span_copy(last + 1, g // (KVH // 2)).wait_recv()
        _, summed, blended = merged(last + 1, 1, g)
        out = (blended / jnp.sum(summed, axis=1, keepdims=True)).astype(jnp.bfloat16)
        for h in range(heads):
            column = (g * heads + h) * HD
            span_rows[:, column : column + HD] = out[h * tokens : (h + 1) * tokens]
        columns = pl.ds(g * heads * HD, heads * HD)
        write = pltpu.make_async_copy(
            span_rows.at[:, columns], span_ref.at[:, columns], out_sems.at[1 + g]
        )
        write.start()
        writes.append(write)
    for write in writes:
        write.wait()
    for k in others:
        patch_copy(k).wait_send()
        for side in range(2):
            span_copy(k, side).wait_send()


def routed(
    devices, patches, row_owner, window_slot, w_patch, vit_gain, w_qkv, queries, new_kv,
    kv_cache, block_table,
):
    src_rows, patch = patches.shape
    vit = w_patch.shape[1]
    inner = VHEADS * VHD
    tokens, width = new_kv.shape
    blocks_dev, block_tokens, _ = kv_cache.shape
    per_owner = 2 * block_table.shape[1] // devices
    keys = devices * per_owner * block_tokens
    rows = QHEADS * tokens
    bf16, f32 = jnp.bfloat16, jnp.float32
    vmem, anywhere = pl.BlockSpec(memory_space=pltpu.VMEM), pl.BlockSpec(memory_space=pl.ANY)
    dma = pltpu.SemaphoreType.DMA
    return pl.pallas_call(
        functools.partial(route_kernel, devices, (vit, blocks_dev, block_tokens, per_owner)),
        out_shape=(
            jax.ShapeDtypeStruct((src_rows, inner), bf16),
            jax.ShapeDtypeStruct(queries.shape, bf16),
        ),
        in_specs=[
            anywhere, anywhere, anywhere, anywhere, anywhere, anywhere, anywhere, anywhere, anywhere, anywhere,
        ],
        out_specs=(anywhere, anywhere),
        scratch_shapes=[
            pltpu.VMEM((1, src_rows), jnp.int32),
            pltpu.VMEM((1, src_rows), jnp.int32),
            pltpu.VMEM(vit_gain.shape, f32),
            pltpu.VMEM(block_table.shape, jnp.int32),
            pltpu.VMEM((devices, patch, src_rows), bf16),
            pltpu.VMEM((patch, vit), bf16),
            pltpu.VMEM((vit, 3 * inner), bf16),
            pltpu.VMEM(kv_cache.shape, bf16),
            pltpu.VMEM((rows, HD), bf16),
            pltpu.VMEM((tokens, width), bf16),
            pltpu.VMEM((devices, 2, HD), jnp.int32),
            pltpu.VMEM((devices * per_owner, HD), jnp.int32),
            pltpu.SMEM((devices * per_owner, HD), jnp.int32),
            pltpu.VMEM((2, keys, width // 2), bf16),
            pltpu.VMEM((2, keys, width // 2), bf16),
            pltpu.VMEM((devices, per_owner, HD), f32),
            pltpu.VMEM((src_rows, inner), bf16),
            pltpu.VMEM((devices * src_rows, 2 * inner), bf16),
            pltpu.VMEM((src_rows, inner), f32),
            pltpu.VMEM((src_rows, inner), bf16),
            pltpu.VMEM(queries.shape, bf16),
            pltpu.VMEM((rows, HD), f32),
            pltpu.VMEM((rows, HD), f32),
            pltpu.VMEM((rows, HD), f32),
            dma((4,)),
            dma((5,)),
            dma((QHEADS,)),
            dma,
        ]
        + [dma((devices,))] * 4
        + [dma((2 * devices,))] * 2
        + [dma((1 + KVH,))],
        compiler_params=pltpu.CompilerParams(
            collective_id=0, has_side_effects=True, vmem_limit_bytes=58 << 20
        ),
        name="route",
    )(
        patches.T, row_owner.reshape(1, src_rows), window_slot.reshape(1, src_rows), w_patch,
        vit_gain, w_qkv, queries, new_kv, kv_cache, block_table,
    )


def place_kernel(a_ref, b_ref, c_ref, d_ref):
    c_ref[...] = a_ref[...]
    d_ref[...] = b_ref[...]


def placed(outs):
    steps = PLACE_STEPS
    specs = tuple(pl.BlockSpec((o.shape[0] // steps, o.shape[1]), lambda i: (i, 0)) for o in outs)
    return pl.pallas_call(
        place_kernel,
        out_shape=tuple(jax.ShapeDtypeStruct(o.shape, o.dtype) for o in outs),
        grid=(steps,),
        in_specs=specs,
        out_specs=specs,
        name="place",
    )(*outs)


def shards(
    patches,
    row_owner,
    window_slot,
    w_patch,
    vit_gain,
    w_qkv,
    queries,
    new_kv,
    kv_cache,
    block_table,
):
    devices = lax.axis_size("seq")
    per_owner = 2 * block_table.shape[1] // devices
    whole_tiles = patches.shape[0] == HD and per_owner == 8 and per_owner * kv_cache.shape[1] == HD
    ordered = devices == 1 + len(EARLY + MIDDLE + LATE)
    if whole_tiles and ordered and new_kv.shape[0] == HD and block_table.shape[1] < HD:
        outs = routed(
            devices, patches, row_owner, window_slot, w_patch, vit_gain, w_qkv, queries,
            new_kv, kv_cache, block_table,
        )
        return placed(outs)
    table_row = block_table[0]
    table_len = table_row.shape[0]
    blocks_dev = kv_cache.shape[0]
    per_owner = max(1, 2 * table_len // devices)
    is_live = table_row >= 0
    holder = jnp.where(is_live, table_row // blocks_dev, -1)
    local_block = jnp.where(is_live, table_row % blocks_dev, 0)
    before_entry = jnp.arange(table_len)[:, None] > jnp.arange(table_len)[None, :]
    same_holder = (holder[:, None] == holder[None, :]) & is_live[None, :] & before_entry
    holder_rank = jnp.sum(same_holder.astype(jnp.int32), axis=1)
    request_slot = jnp.where(is_live, holder * per_owner + holder_rank, devices * per_owner)
    slot_hits = request_slot[:, None] == jnp.arange(devices * per_owner)[None, :]
    wanted = jnp.sum(jnp.where(slot_hits, local_block[:, None], 0), axis=0).astype(jnp.int32)
    asked = lax.all_to_all(
        wanted.reshape(devices, per_owner), "seq", split_axis=0, concat_axis=0, tiled=True
    )
    fetched = kv_cache[asked]
    delivered = lax.all_to_all(fetched, "seq", split_axis=0, concat_axis=0, tiled=True)

    src_rows = patches.shape[0]
    capacity = max(1, 2 * src_rows // devices)
    slot_count = devices * capacity
    owner_ids = row_owner[:, 0]
    owner_hits = (owner_ids[:, None] == jnp.arange(devices)[None, :]).astype(jnp.bfloat16)
    strictly_lower = (jnp.arange(src_rows)[:, None] > jnp.arange(src_rows)[None, :]).astype(
        jnp.bfloat16
    )
    earlier = jnp.dot(strictly_lower, owner_hits, preferred_element_type=jnp.float32)
    ranks = jnp.sum(earlier * owner_hits.astype(jnp.float32), axis=1).astype(jnp.int32)
    target_slot = owner_ids * capacity + ranks
    row_hits = jnp.arange(slot_count)[:, None] == target_slot[None, :]
    window_buffer = jnp.sum(jnp.where(row_hits, window_slot[None, :] + 1, 0), axis=1) - 1
    normed = embed_rows(patches, w_patch, vit_gain)
    outgoing = jnp.dot(
        row_hits.astype(jnp.bfloat16), normed, preferred_element_type=jnp.float32
    ).astype(jnp.bfloat16)
    tag = jnp.broadcast_to(window_buffer.astype(jnp.bfloat16)[:, None], (slot_count, HD))
    outgoing, fetched = lax.optimization_barrier(
        (jnp.concatenate([outgoing, tag], axis=1), fetched)
    )
    arrived = lax.all_to_all(
        outgoing.reshape(devices, capacity, -1), "seq", split_axis=0, concat_axis=0, tiled=True
    ).reshape(slot_count, -1)
    vit = normed.shape[1]
    arrived_windows = arrived[:, vit].astype(jnp.int32)
    qkv_rows = jnp.dot(arrived[:, :vit], w_qkv, preferred_element_type=jnp.float32).astype(
        jnp.bfloat16
    )
    attended = window_attention(qkv_rows, arrived_windows)
    returned = lax.all_to_all(
        attended.reshape(devices, capacity, -1), "seq", split_axis=0, concat_axis=0, tiled=True
    )
    vision_out = jnp.dot(
        row_hits.T.astype(jnp.bfloat16),
        returned.reshape(slot_count, -1),
        preferred_element_type=jnp.float32,
    ).astype(jnp.bfloat16)
    slots = jnp.where(is_live, request_slot, 0).astype(jnp.int32)
    attention_out = prompt_attention(
        queries,
        new_kv,
        delivered.reshape((devices * per_owner,) + kv_cache.shape[1:]),
        slots,
        is_live,
    )
    return (vision_out, attention_out)


def solution(mesh):
    in_specs = (
        P(("groups", "seq"), None),
        P(("groups", "seq"), None),
        P(("groups", "seq")),
        P(),
        P(),
        P(),
        P(("groups", "seq"), None),
        P(("groups", "seq"), None),
        P(("groups", "seq"), None, None),
        P(("groups", "seq"), None),
    )
    out_specs = (P(("groups", "seq"), None), P(("groups", "seq"), None))
    return jax.shard_map(shards, mesh=mesh, in_specs=in_specs, out_specs=out_specs, check_vma=False)
```

```python
import functools

import jax
import jax.numpy as jnp
from jax import lax
from jax.experimental import pallas as pl
from jax.experimental.pallas import tpu as pltpu
from jax.sharding import PartitionSpec as P

VHEADS = 8
VHD = 80
QHEADS = 32
KVH = 4
HD = 128
DEAD = -1e30
EARLY = (8, 9, 1)
MIDDLE = (12, 10, 13, 11)
LATE = (14, 15, 5, 4, 7, 6, 3, 2)
OUTER_ORDER = (0, 6, 1, 7, 4, 2, 3, 5)
INNER_ORDER = (0, 4, 1, 5, 2, 3, 6, 7)


def embed_rows(patch_rows, w_patch, vit_gain):
    embedded = jnp.dot(patch_rows, w_patch, preferred_element_type=jnp.float32).astype(jnp.bfloat16)
    widened = lax.optimization_barrier(embedded).astype(jnp.float32)
    factor = lax.rsqrt(jnp.mean(widened * widened, axis=1, keepdims=True) + 1e-06)
    return (widened * factor * vit_gain).astype(jnp.bfloat16)


def window_attention(qkv_rows, windows):
    total_rows = qkv_rows.shape[0]
    inner_width = VHEADS * VHD
    query_heads = qkv_rows[:, :inner_width].reshape(total_rows, VHEADS, VHD)
    key_heads = qkv_rows[:, inner_width : 2 * inner_width].reshape(total_rows, VHEADS, VHD)
    value_heads = qkv_rows[:, 2 * inner_width :].reshape(total_rows, VHEADS, VHD)
    is_live = windows >= 0
    every_row = jnp.arange(total_rows)
    scores = jnp.einsum(
        "qhd,khd->hqk", query_heads, key_heads, preferred_element_type=jnp.float32
    ) * VHD ** (-0.5)
    allowed = (windows[:, None] == windows[None, :]) & is_live[None, :] | (
        every_row[:, None] == every_row[None, :]
    )
    scores = jnp.where(allowed[None], scores, -jnp.inf)
    highest = jnp.max(scores, axis=2, keepdims=True)
    weights = jnp.exp(scores - highest)
    totals = jnp.sum(weights, axis=2)
    blended = jnp.einsum(
        "hqk,khd->qhd",
        weights.astype(jnp.bfloat16),
        value_heads,
        preferred_element_type=jnp.float32,
    )
    pieces = (blended / totals.T[:, :, None]).reshape(total_rows, inner_width)
    return pieces.astype(jnp.bfloat16)


def span_kernel(slots, q_ref, fresh_ref, bias_ref, kv_ref, o_ref, held, sems):
    tokens = q_ref.shape[0]
    table_len, block_tokens = held.shape[0] - tokens // kv_ref.shape[1], kv_ref.shape[1]
    group_size = QHEADS // KVH
    width = held.shape[2]

    def copy_of(t):
        return pltpu.make_async_copy(kv_ref.at[slots[t]], held.at[t], sems.at[t])

    fresh_copy = pltpu.make_async_copy(
        fresh_ref, held.at[pl.ds(table_len, tokens // block_tokens)], sems.at[table_len]
    )
    fresh_copy.start()
    for t in range(table_len):
        copy_of(t).start()
    for t in range(table_len):
        copy_of(t).wait()
    fresh_copy.wait()
    keys = held.shape[0] * block_tokens
    rows = 2 * tokens
    causal = lax.broadcasted_iota(jnp.int32, (rows, keys), 1) - table_len * block_tokens <= lax.rem(
        lax.broadcasted_iota(jnp.int32, (rows, keys), 0), tokens
    )
    bias = jnp.where(causal, bias_ref[...], DEAD)
    for g in range(KVH):
        key_head = held[:, :, g * HD : (g + 1) * HD].reshape(keys, HD)
        value_head = held[:, :, width // 2 + g * HD : width // 2 + (g + 1) * HD].reshape(keys, HD)
        for pair in range(group_size // 2):
            first = g * group_size + 2 * pair
            query = jnp.concatenate(
                [q_ref[:, (first + i) * HD : (first + i + 1) * HD] for i in range(2)], axis=0
            )
            scores = lax.dot_general(
                query, key_head, (((1,), (1,)), ((), ())), preferred_element_type=jnp.float32
            ) * HD ** (-0.5) + bias
            highest = jnp.max(scores, axis=1, keepdims=True)
            weights = jnp.exp(scores - highest)
            totals = jnp.sum(weights, axis=1, keepdims=True)
            blended = jnp.dot(
                weights.astype(jnp.bfloat16), value_head, preferred_element_type=jnp.float32
            )
            out = (blended / totals).astype(jnp.bfloat16)
            for i in range(2):
                o_ref[:, (first + i) * HD : (first + i + 1) * HD] = out[i * tokens : (i + 1) * tokens]


def prompt_attention(queries, new_kv, delivered, slots, table_live):
    tokens = queries.shape[0]
    table_len = slots.shape[0]
    block_tokens, width = delivered.shape[1:]
    held_blocks = table_len + tokens // block_tokens
    bias = jnp.concatenate(
        [
            jnp.where(jnp.repeat(table_live, block_tokens), 0.0, DEAD),
            jnp.zeros((tokens,), jnp.float32),
        ]
    ).astype(jnp.float32)[None, :]
    return pl.pallas_call(
        span_kernel,
        out_shape=jax.ShapeDtypeStruct(queries.shape, jnp.bfloat16),
        grid_spec=pltpu.PrefetchScalarGridSpec(
            num_scalar_prefetch=1,
            in_specs=[
                pl.BlockSpec(memory_space=pltpu.VMEM),
                pl.BlockSpec(memory_space=pl.ANY),
                pl.BlockSpec(memory_space=pltpu.VMEM),
                pl.BlockSpec(memory_space=pl.ANY),
            ],
            out_specs=pl.BlockSpec(memory_space=pltpu.VMEM),
            scratch_shapes=[
                pltpu.VMEM((held_blocks, block_tokens, width), jnp.bfloat16),
                pltpu.SemaphoreType.DMA((table_len + 1,)),
            ],
        ),
        compiler_params=pltpu.CompilerParams(vmem_limit_bytes=40 << 20),
        name="span",
    )(slots, queries, new_kv.reshape(tokens // block_tokens, block_tokens, width), bias, delivered)


def route_kernel(
    devices,
    scale_dims,
    patches_hbm,
    owner_hbm,
    window_hbm,
    w_patch_hbm,
    gain_hbm,
    w_qkv_hbm,
    queries_hbm,
    fresh_hbm,
    cache_hbm,
    table_hbm,
    vision_ref,
    span_ref,
    owner_ref,
    window_ref,
    gain_ref,
    table_ref,
    patches,
    w_patch,
    w_qkv,
    cache,
    query,
    fresh,
    notes,
    picks,
    picks_smem,
    staged,
    spans,
    span_bias,
    own_query,
    vision_kv,
    pieces,
    vision_rows,
    span_rows,
    top,
    total,
    blend,
    small_sems,
    load_sems,
    query_sems,
    pick_sem,
    note_send,
    note_recv,
    patch_send,
    patch_recv,
    span_send,
    span_recv,
    out_sems,
):
    vit, blocks_dev, block_tokens, per_owner = scale_dims
    me = lax.axis_index("seq")
    tokens = fresh.shape[0]
    src_rows = owner_ref.shape[1]
    chunk = per_owner * block_tokens
    inner = VHEADS * VHD
    group_rows = QHEADS // KVH * tokens
    kv_width = KVH * HD
    part = kv_width // 2
    half = devices // 2
    bits = devices.bit_length() - 1

    def peer(k):
        other = me
        bit = 1
        while bit < devices:
            other = other + bit * ((k // bit) % 2) * (1 - 2 * ((me // bit) % 2))
            bit *= 2
        return other

    def remote(src, dst, send, recv, i, k):
        return pltpu.make_async_remote_copy(
            src_ref=src,
            dst_ref=dst,
            send_sem=send.at[i],
            recv_sem=recv.at[i],
            device_id={"seq": peer(k)},
            device_id_type=pl.DeviceIdType.MESH,
        )

    def note_copy(k):
        return remote(notes.at[0], notes.at[k], note_send, note_recv, k, k)

    def patch_copy(place):
        step = place.bit_length() - 1
        return remote(
            patches.at[place - (1 << step)],
            patches.at[place],
            patch_send,
            patch_recv,
            place,
            devices >> (step + 1),
        )

    def forward(place):
        step = place.bit_length()
        while (1 << step) < devices:
            patch_copy(place + (1 << step)).start()
            step += 1

    def take(place):
        patch_copy(place).wait_recv()
        forward(place)

    def span_copy(k, side):
        base = k * chunk
        rows = pl.ds(base if isinstance(k, int) else pl.multiple_of(base, chunk), chunk)
        i = side * devices + k
        return remote(staged.at[side, rows], spans.at[side, rows], span_send, span_recv, i, k)

    def send_chunk(k):
        for side in range(2):
            span_copy(k, side).start()

    def take_chunk(k):
        for side in range(2):
            span_copy(k, side).wait_recv()

    others = range(1, devices)
    barrier = pltpu.get_barrier_semaphore()
    for k in reversed(others):
        pl.semaphore_signal(
            barrier, inc=1, device_id={"seq": peer(k)}, device_id_type=pl.DeviceIdType.MESH
        )
    small = [
        pltpu.make_async_copy(a, b, small_sems.at[i])
        for i, (a, b) in enumerate(
            (
                (table_hbm, table_ref),
                (owner_hbm, owner_ref),
                (window_hbm, window_ref),
                (gain_hbm, gain_ref),
            )
        )
    ]
    for load in small:
        load.start()
    pairs = (
        (patches_hbm, patches.at[0]),
        (cache_hbm, cache),
        (fresh_hbm, fresh),
        (w_patch_hbm, w_patch),
        (w_qkv_hbm, w_qkv),
    )
    loads = [pltpu.make_async_copy(a, b, load_sems.at[i]) for i, (a, b) in enumerate(pairs)]
    query_loads = [
        pltpu.make_async_copy(
            queries_hbm.at[:, pl.ds(h * HD, HD)],
            query.at[pl.ds(h * tokens, tokens)],
            query_sems.at[h],
        )
        for h in range(QHEADS)
    ]
    for load in loads[:2]:
        load.start()
    for load in small:
        load.wait()
    table = jnp.concatenate(
        [table_ref[...], jnp.full((1, HD - table_ref.shape[1]), -1, jnp.int32)], axis=1
    )
    window_ids = window_ref[...] * devices + owner_ref[...]
    notes[0] = jnp.concatenate([table, window_ids], axis=0)
    pl.semaphore_wait(barrier, devices - 1)
    for k in range(half, devices):
        note_copy(k).start()
    loads[0].wait()
    patch_copy(1).start()
    for k in range(1, half):
        note_copy(k).start()
    for place in (8, 4, 2):
        patch_copy(place).start()
    for load in loads[2:3] + query_loads + loads[3:]:
        load.start()

    for k in others:
        note_copy(k).wait()
    asked = jnp.concatenate(
        [jnp.broadcast_to(notes[k, 0:1], (per_owner, HD)) for k in range(devices)], axis=0
    )
    first = me * blocks_dev
    hits = (asked >= first) & (asked < first + blocks_dev)
    before = (
        lax.broadcasted_iota(jnp.int32, (HD, HD), 0) < lax.broadcasted_iota(jnp.int32, (HD, HD), 1)
    )
    places = jnp.dot(
        jnp.where(hits, 1.0, 0.0).astype(jnp.bfloat16),
        jnp.where(before, 1.0, 0.0).astype(jnp.bfloat16),
        preferred_element_type=jnp.float32,
    ).astype(jnp.int32)
    turn = lax.rem(lax.broadcasted_iota(jnp.int32, asked.shape, 0), per_owner)
    local = jnp.sum(
        jnp.where(hits & (places == turn), (asked - first).astype(jnp.float32), 0.0),
        axis=1,
        keepdims=True,
    ).astype(jnp.int32)
    picks[...] = jnp.broadcast_to(local, picks.shape)
    pick_copy = pltpu.make_async_copy(picks, picks_smem, pick_sem)
    pick_copy.start()
    loads[1].wait()
    pick_copy.wait()

    def gather(k):
        target = staged if k else spans
        for s in range(per_owner):
            pick = jnp.clip(picks_smem[k * per_owner + s, 0], 0, blocks_dev - 1)
            rows = pl.ds(k * chunk + s * block_tokens, block_tokens)
            block = cache[pick]
            for i in range(2):
                first = i * part
                target[i, rows, 0:part] = block[:, first : first + part]
                target[i, rows, part:] = block[:, kv_width + first : kv_width + first + part]

    for k in EARLY + (0,) + MIDDLE + LATE:
        gather(k)
    quarter = me // (devices // 4)
    outer = (quarter == 0) | (quarter == 3)

    for k in EARLY:
        send_chunk(k)
    own = jnp.broadcast_to(table, (per_owner, HD))
    step = lax.broadcasted_iota(jnp.int32, (per_owner, HD), 1)
    for k in range(devices):
        first = peer(k) * blocks_dev
        mine = (own >= first) & (own < first + blocks_dev)
        count = jnp.sum(jnp.where(mine, 1.0, 0.0), axis=1, keepdims=True).astype(jnp.int32)
        span_bias[k] = jnp.where(step < count * block_tokens, 0.0, DEAD)

    flip = (((0,), (0,)), ((), ()))
    contract = (((1,), (1,)), ((), ()))
    loads[2].wait()
    for load in query_loads:
        load.wait()
    causal = lax.rem(
        lax.broadcasted_iota(jnp.int32, (group_rows, tokens), 0), tokens
    ) >= lax.broadcasted_iota(jnp.int32, (group_rows, tokens), 1)
    for g in range(KVH):
        rows = slice(g * group_rows, (g + 1) * group_rows)
        scores = lax.dot_general(
            query[rows], fresh[:, g * HD : (g + 1) * HD], contract, preferred_element_type=jnp.float32
        ) * HD ** (-0.5)
        scores = jnp.where(causal, scores, DEAD)
        highest = jnp.max(scores, axis=1, keepdims=True)
        weights = jnp.exp(scores - highest)
        top[rows] = jnp.broadcast_to(highest, (group_rows, HD))
        total[rows] = weights
        blend[rows] = jnp.dot(
            weights.astype(jnp.bfloat16),
            fresh[:, kv_width + g * HD : kv_width + (g + 1) * HD],
            preferred_element_type=jnp.float32,
        )

    def near_places(offset):
        return [p for p in range(devices) if p % 2 == offset]

    @pl.when(jnp.logical_not(outer))
    def _():
        take(1)

    for place in near_places(0)[1:]:
        take(place)

    @pl.when(outer)
    def _():
        take(1)

    for k in MIDDLE:
        send_chunk(k)

    def embed(i, _):
        place = 0
        for b in range(bits - 1):
            place = place + ((i // (1 << b)) % 2) * (1 << (bits - 2 - b))
        rows = jnp.concatenate([patches[place], patches[place + half]], axis=1)
        embedded = (
            lax.dot_general(rows, w_patch[...], flip, preferred_element_type=jnp.float32)
            .astype(jnp.bfloat16)
            .astype(jnp.float32)
        )
        factor = lax.rsqrt(jnp.mean(embedded * embedded, axis=1, keepdims=True) + 1e-06)
        normed = (embedded * factor * gain_ref[...].reshape(1, vit)).astype(jnp.bfloat16)
        vision_kv[pl.ds(pl.multiple_of(i * 2 * src_rows, 2 * src_rows), 2 * src_rows), :] = jnp.dot(
            normed, w_qkv[:, inner:], preferred_element_type=jnp.float32
        ).astype(jnp.bfloat16)

        @pl.when(i == 0)
        def _():
            own_query[...] = jnp.dot(
                normed[0:src_rows], w_qkv[:, 0:inner], preferred_element_type=jnp.float32
            ).astype(jnp.bfloat16)

        return 0

    def merged(k, width, g):
        base = k * chunk
        bias = jnp.concatenate([span_bias[k + i, 0:1] for i in range(width)], axis=1)
        span = pl.ds(pl.multiple_of(base, chunk), width * chunk)
        side, column = g // (KVH // 2), g % (KVH // 2) * HD
        rows = slice(g * group_rows, (g + 1) * group_rows)
        scores = lax.dot_general(
            query[rows],
            spans[side, span, column : column + HD],
            contract,
            preferred_element_type=jnp.float32,
        ) * HD ** (-0.5) + bias
        old = top[rows]
        highest = jnp.maximum(old, jnp.max(scores, axis=1, keepdims=True))
        shrink = jnp.exp(old - highest)
        parts = [jnp.exp(scores[:, i * chunk : (i + 1) * chunk] - highest) for i in range(width)]
        summed = total[rows] * shrink
        for piece in parts:
            summed = summed + piece
        weights = jnp.concatenate([piece.astype(jnp.bfloat16) for piece in parts], axis=1)
        blended = blend[rows] * shrink + jnp.dot(
            weights,
            spans[side, span, part + column : part + column + HD],
            preferred_element_type=jnp.float32,
        )
        return highest, summed, blended

    def absorb(k, width):
        for g in range(KVH):
            rows = slice(g * group_rows, (g + 1) * group_rows)
            top[rows], total[rows], blend[rows] = merged(k, width, g)

    def pair_at(j):
        pair = 0
        for i, (a, b) in enumerate(zip(OUTER_ORDER, INNER_ORDER)):
            pair = jnp.where(j == i, jnp.where(outer, a, b), pair)
        return 2 * pair

    def absorb_pair(j, _):
        k = pair_at(j)
        take_chunk(k)
        take_chunk(k + 1)
        absorb(k, 2)
        return 0

    loads[3].wait()
    loads[4].wait()
    lax.fori_loop(0, half // 2, embed, 0)
    take(3)
    for k in LATE:
        send_chunk(k)
    take_chunk(1)
    absorb(0, 2)
    take(5)
    lax.fori_loop(1, 2, absorb_pair, 0)
    take(7)
    for place in near_places(1)[4:]:
        take(place)
    lax.fori_loop(half // 2, half, embed, 0)

    keys_ids = []
    for i in range(half):
        place = sum(((i >> b) & 1) << (bits - 2 - b) for b in range(bits - 1))
        for p in (place, place + half):
            k = sum(((p >> b) & 1) << (bits - 1 - b) for b in range(bits))
            keys_ids.append(notes[k, 1:2])
    keys_ids = jnp.concatenate(keys_ids, axis=1).astype(jnp.float32)
    own_ids = jnp.transpose(
        jnp.broadcast_to(window_ids.astype(jnp.float32), (src_rows, src_rows))
    )[:, 0:1]
    same = own_ids == keys_ids
    same = jnp.concatenate([same, same], axis=0)
    columns = lax.broadcasted_iota(jnp.int32, (src_rows, inner), 1)

    def window_heads(pair, _):
        insides = [
            (columns >= h * VHD) & (columns < (h + 1) * VHD) for h in (2 * pair, 2 * pair + 1)
        ]
        wide = own_query[...].astype(jnp.float32)
        stacked = jnp.concatenate(
            [jnp.where(inside, wide, 0.0) for inside in insides], axis=0
        ).astype(jnp.bfloat16)
        scores = lax.dot_general(
            stacked, vision_kv[:, 0:inner], contract, preferred_element_type=jnp.float32
        ) * VHD ** (-0.5)
        scores = jnp.where(same, scores, DEAD)
        weights = jnp.exp(scores - jnp.max(scores, axis=1, keepdims=True))
        totals = jnp.sum(weights, axis=1, keepdims=True)
        blended = (
            jnp.dot(
                weights.astype(jnp.bfloat16), vision_kv[:, inner:], preferred_element_type=jnp.float32
            )
            / totals
        )
        held = pieces[...]
        held = jnp.where(insides[0], blended[0:src_rows], held)
        pieces[...] = jnp.where(insides[1], blended[src_rows:], held)
        return 0

    pieces[...] = jnp.zeros_like(pieces)
    lax.fori_loop(0, VHEADS // 2, window_heads, 0)
    vision_rows[...] = pieces[...].astype(jnp.bfloat16)
    vision_write = pltpu.make_async_copy(vision_rows, vision_ref, out_sems.at[0])
    vision_write.start()
    lax.fori_loop(2, half - 1, absorb_pair, 0)
    last = pair_at(half - 1)
    take_chunk(last)
    absorb(last, 1)
    heads = QHEADS // KVH
    writes = [vision_write]
    for g in range(KVH):
        if g % (KVH // 2) == 0:
            span_copy(last + 1, g // (KVH // 2)).wait_recv()
        _, summed, blended = merged(last + 1, 1, g)
        out = (blended / jnp.sum(summed, axis=1, keepdims=True)).astype(jnp.bfloat16)
        for h in range(heads):
            column = (g * heads + h) * HD
            span_rows[:, column : column + HD] = out[h * tokens : (h + 1) * tokens]
        columns = pl.ds(g * heads * HD, heads * HD)
        write = pltpu.make_async_copy(
            span_rows.at[:, columns], span_ref.at[:, columns], out_sems.at[1 + g]
        )
        write.start()
        writes.append(write)
    for write in writes:
        write.wait()
    for k in others:
        patch_copy(k).wait_send()
        for side in range(2):
            span_copy(k, side).wait_send()


def routed(
    devices, patches, row_owner, window_slot, w_patch, vit_gain, w_qkv, queries, new_kv,
    kv_cache, block_table,
):
    src_rows, patch = patches.shape
    vit = w_patch.shape[1]
    inner = VHEADS * VHD
    tokens, width = new_kv.shape
    blocks_dev, block_tokens, _ = kv_cache.shape
    per_owner = 2 * block_table.shape[1] // devices
    keys = devices * per_owner * block_tokens
    rows = QHEADS * tokens
    bf16, f32 = jnp.bfloat16, jnp.float32
    vmem, anywhere = pl.BlockSpec(memory_space=pltpu.VMEM), pl.BlockSpec(memory_space=pl.ANY)
    dma = pltpu.SemaphoreType.DMA
    return pl.pallas_call(
        functools.partial(route_kernel, devices, (vit, blocks_dev, block_tokens, per_owner)),
        out_shape=(
            jax.ShapeDtypeStruct((src_rows, inner), bf16),
            jax.ShapeDtypeStruct(queries.shape, bf16),
        ),
        in_specs=[
            anywhere, anywhere, anywhere, anywhere, anywhere, anywhere, anywhere, anywhere, anywhere, anywhere,
        ],
        out_specs=(anywhere, anywhere),
        scratch_shapes=[
            pltpu.VMEM((1, src_rows), jnp.int32),
            pltpu.VMEM((1, src_rows), jnp.int32),
            pltpu.VMEM(vit_gain.shape, f32),
            pltpu.VMEM(block_table.shape, jnp.int32),
            pltpu.VMEM((devices, patch, src_rows), bf16),
            pltpu.VMEM((patch, vit), bf16),
            pltpu.VMEM((vit, 3 * inner), bf16),
            pltpu.VMEM(kv_cache.shape, bf16),
            pltpu.VMEM((rows, HD), bf16),
            pltpu.VMEM((tokens, width), bf16),
            pltpu.VMEM((devices, 2, HD), jnp.int32),
            pltpu.VMEM((devices * per_owner, HD), jnp.int32),
            pltpu.SMEM((devices * per_owner, HD), jnp.int32),
            pltpu.VMEM((2, keys, width // 2), bf16),
            pltpu.VMEM((2, keys, width // 2), bf16),
            pltpu.VMEM((devices, per_owner, HD), f32),
            pltpu.VMEM((src_rows, inner), bf16),
            pltpu.VMEM((devices * src_rows, 2 * inner), bf16),
            pltpu.VMEM((src_rows, inner), f32),
            pltpu.VMEM((src_rows, inner), bf16),
            pltpu.VMEM(queries.shape, bf16),
            pltpu.VMEM((rows, HD), f32),
            pltpu.VMEM((rows, HD), f32),
            pltpu.VMEM((rows, HD), f32),
            dma((4,)),
            dma((5,)),
            dma((QHEADS,)),
            dma,
        ]
        + [dma((devices,))] * 4
        + [dma((2 * devices,))] * 2
        + [dma((1 + KVH,))],
        compiler_params=pltpu.CompilerParams(
            collective_id=0, has_side_effects=True, vmem_limit_bytes=52 << 20
        ),
        name="route",
    )(
        *[
            pltpu.with_memory_space_constraint(x, pltpu.HBM)
            for x in (
                patches.T, row_owner.reshape(1, src_rows), window_slot.reshape(1, src_rows), w_patch,
                vit_gain, w_qkv, queries, new_kv, kv_cache, block_table,
            )
        ]
    )


def place_kernel(a_ref, b_ref, c_ref, d_ref):
    c_ref[...] = a_ref[...]
    d_ref[...] = b_ref[...]


def placed(outs):
    steps = PLACE_STEPS
    specs = tuple(pl.BlockSpec((o.shape[0] // steps, o.shape[1]), lambda i: (i, 0)) for o in outs)
    return pl.pallas_call(
        place_kernel,
        out_shape=tuple(jax.ShapeDtypeStruct(o.shape, o.dtype) for o in outs),
        grid=(steps,),
        in_specs=specs,
        out_specs=specs,
        name="place",
    )(*outs)


def shards(
    patches,
    row_owner,
    window_slot,
    w_patch,
    vit_gain,
    w_qkv,
    queries,
    new_kv,
    kv_cache,
    block_table,
):
    devices = lax.axis_size("seq")
    per_owner = 2 * block_table.shape[1] // devices
    whole_tiles = patches.shape[0] == HD and per_owner == 8 and per_owner * kv_cache.shape[1] == HD
    ordered = devices == 1 + len(EARLY + MIDDLE + LATE)
    if whole_tiles and ordered and new_kv.shape[0] == HD and block_table.shape[1] < HD:
        outs = routed(
            devices, patches, row_owner, window_slot, w_patch, vit_gain, w_qkv, queries,
            new_kv, kv_cache, block_table,
        )
        return outs
    table_row = block_table[0]
    table_len = table_row.shape[0]
    blocks_dev = kv_cache.shape[0]
    per_owner = max(1, 2 * table_len // devices)
    is_live = table_row >= 0
    holder = jnp.where(is_live, table_row // blocks_dev, -1)
    local_block = jnp.where(is_live, table_row % blocks_dev, 0)
    before_entry = jnp.arange(table_len)[:, None] > jnp.arange(table_len)[None, :]
    same_holder = (holder[:, None] == holder[None, :]) & is_live[None, :] & before_entry
    holder_rank = jnp.sum(same_holder.astype(jnp.int32), axis=1)
    request_slot = jnp.where(is_live, holder * per_owner + holder_rank, devices * per_owner)
    slot_hits = request_slot[:, None] == jnp.arange(devices * per_owner)[None, :]
    wanted = jnp.sum(jnp.where(slot_hits, local_block[:, None], 0), axis=0).astype(jnp.int32)
    asked = lax.all_to_all(
        wanted.reshape(devices, per_owner), "seq", split_axis=0, concat_axis=0, tiled=True
    )
    fetched = kv_cache[asked]
    delivered = lax.all_to_all(fetched, "seq", split_axis=0, concat_axis=0, tiled=True)

    src_rows = patches.shape[0]
    capacity = max(1, 2 * src_rows // devices)
    slot_count = devices * capacity
    owner_ids = row_owner[:, 0]
    owner_hits = (owner_ids[:, None] == jnp.arange(devices)[None, :]).astype(jnp.bfloat16)
    strictly_lower = (jnp.arange(src_rows)[:, None] > jnp.arange(src_rows)[None, :]).astype(
        jnp.bfloat16
    )
    earlier = jnp.dot(strictly_lower, owner_hits, preferred_element_type=jnp.float32)
    ranks = jnp.sum(earlier * owner_hits.astype(jnp.float32), axis=1).astype(jnp.int32)
    target_slot = owner_ids * capacity + ranks
    row_hits = jnp.arange(slot_count)[:, None] == target_slot[None, :]
    window_buffer = jnp.sum(jnp.where(row_hits, window_slot[None, :] + 1, 0), axis=1) - 1
    normed = embed_rows(patches, w_patch, vit_gain)
    outgoing = jnp.dot(
        row_hits.astype(jnp.bfloat16), normed, preferred_element_type=jnp.float32
    ).astype(jnp.bfloat16)
    tag = jnp.broadcast_to(window_buffer.astype(jnp.bfloat16)[:, None], (slot_count, HD))
    outgoing, fetched = lax.optimization_barrier(
        (jnp.concatenate([outgoing, tag], axis=1), fetched)
    )
    arrived = lax.all_to_all(
        outgoing.reshape(devices, capacity, -1), "seq", split_axis=0, concat_axis=0, tiled=True
    ).reshape(slot_count, -1)
    vit = normed.shape[1]
    arrived_windows = arrived[:, vit].astype(jnp.int32)
    qkv_rows = jnp.dot(arrived[:, :vit], w_qkv, preferred_element_type=jnp.float32).astype(
        jnp.bfloat16
    )
    attended = window_attention(qkv_rows, arrived_windows)
    returned = lax.all_to_all(
        attended.reshape(devices, capacity, -1), "seq", split_axis=0, concat_axis=0, tiled=True
    )
    vision_out = jnp.dot(
        row_hits.T.astype(jnp.bfloat16),
        returned.reshape(slot_count, -1),
        preferred_element_type=jnp.float32,
    ).astype(jnp.bfloat16)
    slots = jnp.where(is_live, request_slot, 0).astype(jnp.int32)
    attention_out = prompt_attention(
        queries,
        new_kv,
        delivered.reshape((devices * per_owner,) + kv_cache.shape[1:]),
        slots,
        is_live,
    )
    return (vision_out, attention_out)


def solution(mesh):
    in_specs = (
        P(("groups", "seq"), None),
        P(("groups", "seq"), None),
        P(("groups", "seq")),
        P(),
        P(),
        P(),
        P(("groups", "seq"), None),
        P(("groups", "seq"), None),
        P(("groups", "seq"), None, None),
        P(("groups", "seq"), None),
    )
    out_specs = (P(("groups", "seq"), None), P(("groups", "seq"), None))
    return jax.shard_map(shards, mesh=mesh, in_specs=in_specs, out_specs=out_specs, check_vma=False)
```

```python
import functools

import jax
import jax.numpy as jnp
from jax import lax
from jax.experimental import pallas as pl
from jax.experimental.pallas import tpu as pltpu
from jax.sharding import PartitionSpec as P

VHEADS = 8
VHD = 80
QHEADS = 32
KVH = 4
HD = 128
DEAD = -1e30
EARLY = (8, 9, 12, 1)
MIDDLE = (10, 13, 11)
LATE = (14, 15, 5, 4, 7, 6, 3, 2)
OUTER_ORDER = (0, 6, 1, 7, 4, 2, 3, 5)
INNER_ORDER = (0, 4, 1, 5, 2, 3, 6, 7)


def embed_rows(patch_rows, w_patch, vit_gain):
    embedded = jnp.dot(patch_rows, w_patch, preferred_element_type=jnp.float32).astype(jnp.bfloat16)
    widened = lax.optimization_barrier(embedded).astype(jnp.float32)
    factor = lax.rsqrt(jnp.mean(widened * widened, axis=1, keepdims=True) + 1e-06)
    return (widened * factor * vit_gain).astype(jnp.bfloat16)


def window_attention(qkv_rows, windows):
    total_rows = qkv_rows.shape[0]
    inner_width = VHEADS * VHD
    query_heads = qkv_rows[:, :inner_width].reshape(total_rows, VHEADS, VHD)
    key_heads = qkv_rows[:, inner_width : 2 * inner_width].reshape(total_rows, VHEADS, VHD)
    value_heads = qkv_rows[:, 2 * inner_width :].reshape(total_rows, VHEADS, VHD)
    is_live = windows >= 0
    every_row = jnp.arange(total_rows)
    scores = jnp.einsum(
        "qhd,khd->hqk", query_heads, key_heads, preferred_element_type=jnp.float32
    ) * VHD ** (-0.5)
    allowed = (windows[:, None] == windows[None, :]) & is_live[None, :] | (
        every_row[:, None] == every_row[None, :]
    )
    scores = jnp.where(allowed[None], scores, -jnp.inf)
    highest = jnp.max(scores, axis=2, keepdims=True)
    weights = jnp.exp(scores - highest)
    totals = jnp.sum(weights, axis=2)
    blended = jnp.einsum(
        "hqk,khd->qhd",
        weights.astype(jnp.bfloat16),
        value_heads,
        preferred_element_type=jnp.float32,
    )
    pieces = (blended / totals.T[:, :, None]).reshape(total_rows, inner_width)
    return pieces.astype(jnp.bfloat16)


def span_kernel(slots, q_ref, fresh_ref, bias_ref, kv_ref, o_ref, held, sems):
    tokens = q_ref.shape[0]
    table_len, block_tokens = held.shape[0] - tokens // kv_ref.shape[1], kv_ref.shape[1]
    group_size = QHEADS // KVH
    width = held.shape[2]

    def copy_of(t):
        return pltpu.make_async_copy(kv_ref.at[slots[t]], held.at[t], sems.at[t])

    fresh_copy = pltpu.make_async_copy(
        fresh_ref, held.at[pl.ds(table_len, tokens // block_tokens)], sems.at[table_len]
    )
    fresh_copy.start()
    for t in range(table_len):
        copy_of(t).start()
    for t in range(table_len):
        copy_of(t).wait()
    fresh_copy.wait()
    keys = held.shape[0] * block_tokens
    rows = 2 * tokens
    causal = lax.broadcasted_iota(jnp.int32, (rows, keys), 1) - table_len * block_tokens <= lax.rem(
        lax.broadcasted_iota(jnp.int32, (rows, keys), 0), tokens
    )
    bias = jnp.where(causal, bias_ref[...], DEAD)
    for g in range(KVH):
        key_head = held[:, :, g * HD : (g + 1) * HD].reshape(keys, HD)
        value_head = held[:, :, width // 2 + g * HD : width // 2 + (g + 1) * HD].reshape(keys, HD)
        for pair in range(group_size // 2):
            first = g * group_size + 2 * pair
            query = jnp.concatenate(
                [q_ref[:, (first + i) * HD : (first + i + 1) * HD] for i in range(2)], axis=0
            )
            scores = lax.dot_general(
                query, key_head, (((1,), (1,)), ((), ())), preferred_element_type=jnp.float32
            ) * HD ** (-0.5) + bias
            highest = jnp.max(scores, axis=1, keepdims=True)
            weights = jnp.exp(scores - highest)
            totals = jnp.sum(weights, axis=1, keepdims=True)
            blended = jnp.dot(
                weights.astype(jnp.bfloat16), value_head, preferred_element_type=jnp.float32
            )
            out = (blended / totals).astype(jnp.bfloat16)
            for i in range(2):
                o_ref[:, (first + i) * HD : (first + i + 1) * HD] = out[i * tokens : (i + 1) * tokens]


def prompt_attention(queries, new_kv, delivered, slots, table_live):
    tokens = queries.shape[0]
    table_len = slots.shape[0]
    block_tokens, width = delivered.shape[1:]
    held_blocks = table_len + tokens // block_tokens
    bias = jnp.concatenate(
        [
            jnp.where(jnp.repeat(table_live, block_tokens), 0.0, DEAD),
            jnp.zeros((tokens,), jnp.float32),
        ]
    ).astype(jnp.float32)[None, :]
    return pl.pallas_call(
        span_kernel,
        out_shape=jax.ShapeDtypeStruct(queries.shape, jnp.bfloat16),
        grid_spec=pltpu.PrefetchScalarGridSpec(
            num_scalar_prefetch=1,
            in_specs=[
                pl.BlockSpec(memory_space=pltpu.VMEM),
                pl.BlockSpec(memory_space=pl.ANY),
                pl.BlockSpec(memory_space=pltpu.VMEM),
                pl.BlockSpec(memory_space=pl.ANY),
            ],
            out_specs=pl.BlockSpec(memory_space=pltpu.VMEM),
            scratch_shapes=[
                pltpu.VMEM((held_blocks, block_tokens, width), jnp.bfloat16),
                pltpu.SemaphoreType.DMA((table_len + 1,)),
            ],
        ),
        compiler_params=pltpu.CompilerParams(vmem_limit_bytes=40 << 20),
        name="span",
    )(slots, queries, new_kv.reshape(tokens // block_tokens, block_tokens, width), bias, delivered)


def route_kernel(
    devices,
    scale_dims,
    patches_hbm,
    owner_hbm,
    window_hbm,
    w_patch_hbm,
    gain_hbm,
    w_qkv_hbm,
    queries_hbm,
    fresh_hbm,
    cache_hbm,
    table_hbm,
    vision_ref,
    span_ref,
    owner_ref,
    window_ref,
    gain_ref,
    table_ref,
    patches,
    w_patch,
    w_qkv,
    cache,
    query,
    fresh,
    notes,
    picks,
    picks_smem,
    staged,
    spans,
    span_bias,
    own_query,
    vision_kv,
    pieces,
    vision_rows,
    span_rows,
    top,
    total,
    blend,
    small_sems,
    load_sems,
    query_sems,
    pick_sem,
    note_send,
    note_recv,
    patch_send,
    patch_recv,
    span_send,
    span_recv,
    out_sems,
):
    vit, blocks_dev, block_tokens, per_owner = scale_dims
    me = lax.axis_index("seq")
    tokens = fresh.shape[0]
    src_rows = owner_ref.shape[1]
    chunk = per_owner * block_tokens
    inner = VHEADS * VHD
    group_rows = QHEADS // KVH * tokens
    kv_width = KVH * HD
    part = kv_width // 2
    half = devices // 2
    bits = devices.bit_length() - 1

    def peer(k):
        other = me
        bit = 1
        while bit < devices:
            other = other + bit * ((k // bit) % 2) * (1 - 2 * ((me // bit) % 2))
            bit *= 2
        return other

    def remote(src, dst, send, recv, i, k):
        return pltpu.make_async_remote_copy(
            src_ref=src,
            dst_ref=dst,
            send_sem=send.at[i],
            recv_sem=recv.at[i],
            device_id={"seq": peer(k)},
            device_id_type=pl.DeviceIdType.MESH,
        )

    def note_copy(k):
        return remote(notes.at[0], notes.at[k], note_send, note_recv, k, k)

    def patch_copy(place):
        step = place.bit_length() - 1
        return remote(
            patches.at[place - (1 << step)],
            patches.at[place],
            patch_send,
            patch_recv,
            place,
            devices >> (step + 1),
        )

    def forward(place):
        step = place.bit_length()
        while (1 << step) < devices:
            patch_copy(place + (1 << step)).start()
            step += 1

    def take(place):
        patch_copy(place).wait_recv()
        forward(place)

    def span_copy(k, side):
        base = k * chunk
        rows = pl.ds(base if isinstance(k, int) else pl.multiple_of(base, chunk), chunk)
        i = side * devices + k
        return remote(staged.at[side, rows], spans.at[side, rows], span_send, span_recv, i, k)

    def send_chunk(k):
        for side in range(2):
            span_copy(k, side).start()

    def take_chunk(k):
        for side in range(2):
            span_copy(k, side).wait_recv()

    others = range(1, devices)
    barrier = pltpu.get_barrier_semaphore()
    for k in reversed(others):
        pl.semaphore_signal(
            barrier, inc=1, device_id={"seq": peer(k)}, device_id_type=pl.DeviceIdType.MESH
        )
    small = [
        pltpu.make_async_copy(a, b, small_sems.at[i])
        for i, (a, b) in enumerate(
            (
                (table_hbm, table_ref),
                (owner_hbm, owner_ref),
                (window_hbm, window_ref),
                (gain_hbm, gain_ref),
            )
        )
    ]
    for load in small:
        load.start()
    pairs = (
        (patches_hbm, patches.at[0]),
        (cache_hbm, cache),
        (fresh_hbm, fresh),
        (w_patch_hbm, w_patch),
        (w_qkv_hbm, w_qkv),
    )
    loads = [pltpu.make_async_copy(a, b, load_sems.at[i]) for i, (a, b) in enumerate(pairs)]
    query_loads = [
        pltpu.make_async_copy(
            queries_hbm.at[:, pl.ds(h * HD, HD)],
            query.at[pl.ds(h * tokens, tokens)],
            query_sems.at[h],
        )
        for h in range(QHEADS)
    ]
    for load in loads[:2]:
        load.start()
    for load in small:
        load.wait()
    table = jnp.concatenate(
        [table_ref[...], jnp.full((1, HD - table_ref.shape[1]), -1, jnp.int32)], axis=1
    )
    window_ids = window_ref[...] * devices + owner_ref[...]
    notes[0] = jnp.concatenate([table, window_ids], axis=0)
    pl.semaphore_wait(barrier, devices - 1)
    for k in range(half, devices):
        note_copy(k).start()
    loads[0].wait()
    patch_copy(1).start()
    for k in range(1, half):
        note_copy(k).start()
    for place in (8, 4, 2):
        patch_copy(place).start()
    for load in loads[2:3] + query_loads + loads[3:]:
        load.start()

    for k in others:
        note_copy(k).wait()
    asked = jnp.concatenate(
        [jnp.broadcast_to(notes[k, 0:1], (per_owner, HD)) for k in range(devices)], axis=0
    )
    first = me * blocks_dev
    hits = (asked >= first) & (asked < first + blocks_dev)
    before = (
        lax.broadcasted_iota(jnp.int32, (HD, HD), 0) < lax.broadcasted_iota(jnp.int32, (HD, HD), 1)
    )
    places = jnp.dot(
        jnp.where(hits, 1.0, 0.0).astype(jnp.bfloat16),
        jnp.where(before, 1.0, 0.0).astype(jnp.bfloat16),
        preferred_element_type=jnp.float32,
    ).astype(jnp.int32)
    turn = lax.rem(lax.broadcasted_iota(jnp.int32, asked.shape, 0), per_owner)
    local = jnp.sum(
        jnp.where(hits & (places == turn), (asked - first).astype(jnp.float32), 0.0),
        axis=1,
        keepdims=True,
    ).astype(jnp.int32)
    picks[...] = jnp.broadcast_to(local, picks.shape)
    pick_copy = pltpu.make_async_copy(picks, picks_smem, pick_sem)
    pick_copy.start()
    loads[1].wait()
    pick_copy.wait()

    def gather(k):
        target = staged if k else spans
        for s in range(per_owner):
            pick = jnp.clip(picks_smem[k * per_owner + s, 0], 0, blocks_dev - 1)
            rows = pl.ds(k * chunk + s * block_tokens, block_tokens)
            block = cache[pick]
            for i in range(2):
                first = i * part
                target[i, rows, 0:part] = block[:, first : first + part]
                target[i, rows, part:] = block[:, kv_width + first : kv_width + first + part]

    for k in EARLY + (0,) + MIDDLE + LATE:
        gather(k)
    quarter = me // (devices // 4)
    outer = (quarter == 0) | (quarter == 3)

    for k in EARLY:
        send_chunk(k)
    own = jnp.broadcast_to(table, (per_owner, HD))
    step = lax.broadcasted_iota(jnp.int32, (per_owner, HD), 1)
    for k in range(devices):
        first = peer(k) * blocks_dev
        mine = (own >= first) & (own < first + blocks_dev)
        count = jnp.sum(jnp.where(mine, 1.0, 0.0), axis=1, keepdims=True).astype(jnp.int32)
        span_bias[k] = jnp.where(step < count * block_tokens, 0.0, DEAD)

    flip = (((0,), (0,)), ((), ()))
    contract = (((1,), (1,)), ((), ()))
    loads[2].wait()
    for load in query_loads:
        load.wait()
    causal = lax.rem(
        lax.broadcasted_iota(jnp.int32, (group_rows, tokens), 0), tokens
    ) >= lax.broadcasted_iota(jnp.int32, (group_rows, tokens), 1)
    for g in range(KVH):
        rows = slice(g * group_rows, (g + 1) * group_rows)
        scores = lax.dot_general(
            query[rows], fresh[:, g * HD : (g + 1) * HD], contract, preferred_element_type=jnp.float32
        ) * HD ** (-0.5)
        scores = jnp.where(causal, scores, DEAD)
        highest = jnp.max(scores, axis=1, keepdims=True)
        weights = jnp.exp(scores - highest)
        top[rows] = jnp.broadcast_to(highest, (group_rows, HD))
        total[rows] = weights
        blend[rows] = jnp.dot(
            weights.astype(jnp.bfloat16),
            fresh[:, kv_width + g * HD : kv_width + (g + 1) * HD],
            preferred_element_type=jnp.float32,
        )

    def near_places(offset):
        return [p for p in range(devices) if p % 2 == offset]

    @pl.when(jnp.logical_not(outer))
    def _():
        take(1)

    for place in near_places(0)[1:]:
        take(place)

    @pl.when(outer)
    def _():
        take(1)

    for k in MIDDLE:
        send_chunk(k)

    def embed(i, _):
        place = 0
        for b in range(bits - 1):
            place = place + ((i // (1 << b)) % 2) * (1 << (bits - 2 - b))
        rows = jnp.concatenate([patches[place], patches[place + half]], axis=1)
        embedded = (
            lax.dot_general(rows, w_patch[...], flip, preferred_element_type=jnp.float32)
            .astype(jnp.bfloat16)
            .astype(jnp.float32)
        )
        factor = lax.rsqrt(jnp.mean(embedded * embedded, axis=1, keepdims=True) + 1e-06)
        normed = (embedded * factor * gain_ref[...].reshape(1, vit)).astype(jnp.bfloat16)
        vision_kv[pl.ds(pl.multiple_of(i * 2 * src_rows, 2 * src_rows), 2 * src_rows), :] = jnp.dot(
            normed, w_qkv[:, inner:], preferred_element_type=jnp.float32
        ).astype(jnp.bfloat16)

        @pl.when(i == 0)
        def _():
            own_query[...] = jnp.dot(
                normed[0:src_rows], w_qkv[:, 0:inner], preferred_element_type=jnp.float32
            ).astype(jnp.bfloat16)

        return 0

    def merged(k, width, g):
        base = k * chunk
        bias = jnp.concatenate([span_bias[k + i, 0:1] for i in range(width)], axis=1)
        span = pl.ds(pl.multiple_of(base, chunk), width * chunk)
        side, column = g // (KVH // 2), g % (KVH // 2) * HD
        rows = slice(g * group_rows, (g + 1) * group_rows)
        scores = lax.dot_general(
            query[rows],
            spans[side, span, column : column + HD],
            contract,
            preferred_element_type=jnp.float32,
        ) * HD ** (-0.5) + bias
        old = top[rows]
        highest = jnp.maximum(old, jnp.max(scores, axis=1, keepdims=True))
        shrink = jnp.exp(old - highest)
        parts = [jnp.exp(scores[:, i * chunk : (i + 1) * chunk] - highest) for i in range(width)]
        summed = total[rows] * shrink
        for piece in parts:
            summed = summed + piece
        weights = jnp.concatenate([piece.astype(jnp.bfloat16) for piece in parts], axis=1)
        blended = blend[rows] * shrink + jnp.dot(
            weights,
            spans[side, span, part + column : part + column + HD],
            preferred_element_type=jnp.float32,
        )
        return highest, summed, blended

    def absorb(k, width):
        for g in range(KVH):
            rows = slice(g * group_rows, (g + 1) * group_rows)
            top[rows], total[rows], blend[rows] = merged(k, width, g)

    def pair_at(j):
        pair = 0
        for i, (a, b) in enumerate(zip(OUTER_ORDER, INNER_ORDER)):
            pair = jnp.where(j == i, jnp.where(outer, a, b), pair)
        return 2 * pair

    def absorb_pair(j, _):
        k = pair_at(j)
        take_chunk(k)
        take_chunk(k + 1)
        absorb(k, 2)
        return 0

    loads[3].wait()
    loads[4].wait()
    lax.fori_loop(0, half // 2, embed, 0)
    take(3)
    for k in LATE:
        send_chunk(k)
    take_chunk(1)
    absorb(0, 2)
    take(5)
    lax.fori_loop(1, 2, absorb_pair, 0)
    take(7)
    for place in near_places(1)[4:]:
        take(place)
    lax.fori_loop(half // 2, half, embed, 0)

    keys_ids = []
    for i in range(half):
        place = sum(((i >> b) & 1) << (bits - 2 - b) for b in range(bits - 1))
        for p in (place, place + half):
            k = sum(((p >> b) & 1) << (bits - 1 - b) for b in range(bits))
            keys_ids.append(notes[k, 1:2])
    keys_ids = jnp.concatenate(keys_ids, axis=1).astype(jnp.float32)
    own_ids = jnp.transpose(
        jnp.broadcast_to(window_ids.astype(jnp.float32), (src_rows, src_rows))
    )[:, 0:1]
    same = own_ids == keys_ids
    same = jnp.concatenate([same, same], axis=0)
    columns = lax.broadcasted_iota(jnp.int32, (src_rows, inner), 1)

    def window_heads(pair, _):
        insides = [
            (columns >= h * VHD) & (columns < (h + 1) * VHD) for h in (2 * pair, 2 * pair + 1)
        ]
        wide = own_query[...].astype(jnp.float32)
        stacked = jnp.concatenate(
            [jnp.where(inside, wide, 0.0) for inside in insides], axis=0
        ).astype(jnp.bfloat16)
        scores = lax.dot_general(
            stacked, vision_kv[:, 0:inner], contract, preferred_element_type=jnp.float32
        ) * VHD ** (-0.5)
        scores = jnp.where(same, scores, DEAD)
        weights = jnp.exp(scores - jnp.max(scores, axis=1, keepdims=True))
        totals = jnp.sum(weights, axis=1, keepdims=True)
        blended = (
            jnp.dot(
                weights.astype(jnp.bfloat16), vision_kv[:, inner:], preferred_element_type=jnp.float32
            )
            / totals
        )
        held = pieces[...]
        held = jnp.where(insides[0], blended[0:src_rows], held)
        pieces[...] = jnp.where(insides[1], blended[src_rows:], held)
        return 0

    pieces[...] = jnp.zeros_like(pieces)
    lax.fori_loop(0, VHEADS // 2, window_heads, 0)
    vision_rows[...] = pieces[...].astype(jnp.bfloat16)
    vision_write = pltpu.make_async_copy(vision_rows, vision_ref, out_sems.at[0])
    vision_write.start()
    lax.fori_loop(2, half - 1, absorb_pair, 0)
    last = pair_at(half - 1)
    take_chunk(last)
    absorb(last, 1)
    heads = QHEADS // KVH
    writes = [vision_write]
    for g in range(KVH):
        if g % (KVH // 2) == 0:
            span_copy(last + 1, g // (KVH // 2)).wait_recv()
        _, summed, blended = merged(last + 1, 1, g)
        out = (blended / jnp.sum(summed, axis=1, keepdims=True)).astype(jnp.bfloat16)
        for h in range(heads):
            column = (g * heads + h) * HD
            span_rows[:, column : column + HD] = out[h * tokens : (h + 1) * tokens]
        columns = pl.ds(g * heads * HD, heads * HD)
        write = pltpu.make_async_copy(
            span_rows.at[:, columns], span_ref.at[:, columns], out_sems.at[1 + g]
        )
        write.start()
        writes.append(write)
    for write in writes:
        write.wait()
    for k in others:
        patch_copy(k).wait_send()
        for side in range(2):
            span_copy(k, side).wait_send()


def routed(
    devices, patches, row_owner, window_slot, w_patch, vit_gain, w_qkv, queries, new_kv,
    kv_cache, block_table,
):
    src_rows, patch = patches.shape
    vit = w_patch.shape[1]
    inner = VHEADS * VHD
    tokens, width = new_kv.shape
    blocks_dev, block_tokens, _ = kv_cache.shape
    per_owner = 2 * block_table.shape[1] // devices
    keys = devices * per_owner * block_tokens
    rows = QHEADS * tokens
    bf16, f32 = jnp.bfloat16, jnp.float32
    vmem, anywhere = pl.BlockSpec(memory_space=pltpu.VMEM), pl.BlockSpec(memory_space=pl.ANY)
    dma = pltpu.SemaphoreType.DMA
    return pl.pallas_call(
        functools.partial(route_kernel, devices, (vit, blocks_dev, block_tokens, per_owner)),
        out_shape=(
            jax.ShapeDtypeStruct((src_rows, inner), bf16),
            jax.ShapeDtypeStruct(queries.shape, bf16),
        ),
        in_specs=[
            anywhere, anywhere, anywhere, anywhere, anywhere, anywhere, anywhere, anywhere, anywhere, anywhere,
        ],
        out_specs=(anywhere, anywhere),
        scratch_shapes=[
            pltpu.VMEM((1, src_rows), jnp.int32),
            pltpu.VMEM((1, src_rows), jnp.int32),
            pltpu.VMEM(vit_gain.shape, f32),
            pltpu.VMEM(block_table.shape, jnp.int32),
            pltpu.VMEM((devices, patch, src_rows), bf16),
            pltpu.VMEM((patch, vit), bf16),
            pltpu.VMEM((vit, 3 * inner), bf16),
            pltpu.VMEM(kv_cache.shape, bf16),
            pltpu.VMEM((rows, HD), bf16),
            pltpu.VMEM((tokens, width), bf16),
            pltpu.VMEM((devices, 2, HD), jnp.int32),
            pltpu.VMEM((devices * per_owner, HD), jnp.int32),
            pltpu.SMEM((devices * per_owner, HD), jnp.int32),
            pltpu.VMEM((2, keys, width // 2), bf16),
            pltpu.VMEM((2, keys, width // 2), bf16),
            pltpu.VMEM((devices, per_owner, HD), f32),
            pltpu.VMEM((src_rows, inner), bf16),
            pltpu.VMEM((devices * src_rows, 2 * inner), bf16),
            pltpu.VMEM((src_rows, inner), f32),
            pltpu.VMEM((src_rows, inner), bf16),
            pltpu.VMEM(queries.shape, bf16),
            pltpu.VMEM((rows, HD), f32),
            pltpu.VMEM((rows, HD), f32),
            pltpu.VMEM((rows, HD), f32),
            dma((4,)),
            dma((5,)),
            dma((QHEADS,)),
            dma,
        ]
        + [dma((devices,))] * 4
        + [dma((2 * devices,))] * 2
        + [dma((1 + KVH,))],
        compiler_params=pltpu.CompilerParams(
            collective_id=0, has_side_effects=True, vmem_limit_bytes=48 << 20
        ),
        name="route",
    )(
        *[
            pltpu.with_memory_space_constraint(x, pltpu.HBM)
            for x in (
                patches.T, row_owner.reshape(1, src_rows), window_slot.reshape(1, src_rows), w_patch,
                vit_gain, w_qkv, queries, new_kv, kv_cache, block_table,
            )
        ]
    )


def shards(
    patches,
    row_owner,
    window_slot,
    w_patch,
    vit_gain,
    w_qkv,
    queries,
    new_kv,
    kv_cache,
    block_table,
):
    devices = lax.axis_size("seq")
    per_owner = 2 * block_table.shape[1] // devices
    whole_tiles = patches.shape[0] == HD and per_owner == 8 and per_owner * kv_cache.shape[1] == HD
    ordered = devices == 1 + len(EARLY + MIDDLE + LATE)
    if whole_tiles and ordered and new_kv.shape[0] == HD and block_table.shape[1] < HD:
        outs = routed(
            devices, patches, row_owner, window_slot, w_patch, vit_gain, w_qkv, queries,
            new_kv, kv_cache, block_table,
        )
        return outs
    table_row = block_table[0]
    table_len = table_row.shape[0]
    blocks_dev = kv_cache.shape[0]
    per_owner = max(1, 2 * table_len // devices)
    is_live = table_row >= 0
    holder = jnp.where(is_live, table_row // blocks_dev, -1)
    local_block = jnp.where(is_live, table_row % blocks_dev, 0)
    before_entry = jnp.arange(table_len)[:, None] > jnp.arange(table_len)[None, :]
    same_holder = (holder[:, None] == holder[None, :]) & is_live[None, :] & before_entry
    holder_rank = jnp.sum(same_holder.astype(jnp.int32), axis=1)
    request_slot = jnp.where(is_live, holder * per_owner + holder_rank, devices * per_owner)
    slot_hits = request_slot[:, None] == jnp.arange(devices * per_owner)[None, :]
    wanted = jnp.sum(jnp.where(slot_hits, local_block[:, None], 0), axis=0).astype(jnp.int32)
    asked = lax.all_to_all(
        wanted.reshape(devices, per_owner), "seq", split_axis=0, concat_axis=0, tiled=True
    )
    fetched = kv_cache[asked]
    delivered = lax.all_to_all(fetched, "seq", split_axis=0, concat_axis=0, tiled=True)

    src_rows = patches.shape[0]
    capacity = max(1, 2 * src_rows // devices)
    slot_count = devices * capacity
    owner_ids = row_owner[:, 0]
    owner_hits = (owner_ids[:, None] == jnp.arange(devices)[None, :]).astype(jnp.bfloat16)
    strictly_lower = (jnp.arange(src_rows)[:, None] > jnp.arange(src_rows)[None, :]).astype(
        jnp.bfloat16
    )
    earlier = jnp.dot(strictly_lower, owner_hits, preferred_element_type=jnp.float32)
    ranks = jnp.sum(earlier * owner_hits.astype(jnp.float32), axis=1).astype(jnp.int32)
    target_slot = owner_ids * capacity + ranks
    row_hits = jnp.arange(slot_count)[:, None] == target_slot[None, :]
    window_buffer = jnp.sum(jnp.where(row_hits, window_slot[None, :] + 1, 0), axis=1) - 1
    normed = embed_rows(patches, w_patch, vit_gain)
    outgoing = jnp.dot(
        row_hits.astype(jnp.bfloat16), normed, preferred_element_type=jnp.float32
    ).astype(jnp.bfloat16)
    tag = jnp.broadcast_to(window_buffer.astype(jnp.bfloat16)[:, None], (slot_count, HD))
    outgoing, fetched = lax.optimization_barrier(
        (jnp.concatenate([outgoing, tag], axis=1), fetched)
    )
    arrived = lax.all_to_all(
        outgoing.reshape(devices, capacity, -1), "seq", split_axis=0, concat_axis=0, tiled=True
    ).reshape(slot_count, -1)
    vit = normed.shape[1]
    arrived_windows = arrived[:, vit].astype(jnp.int32)
    qkv_rows = jnp.dot(arrived[:, :vit], w_qkv, preferred_element_type=jnp.float32).astype(
        jnp.bfloat16
    )
    attended = window_attention(qkv_rows, arrived_windows)
    returned = lax.all_to_all(
        attended.reshape(devices, capacity, -1), "seq", split_axis=0, concat_axis=0, tiled=True
    )
    vision_out = jnp.dot(
        row_hits.T.astype(jnp.bfloat16),
        returned.reshape(slot_count, -1),
        preferred_element_type=jnp.float32,
    ).astype(jnp.bfloat16)
    slots = jnp.where(is_live, request_slot, 0).astype(jnp.int32)
    attention_out = prompt_attention(
        queries,
        new_kv,
        delivered.reshape((devices * per_owner,) + kv_cache.shape[1:]),
        slots,
        is_live,
    )
    return (vision_out, attention_out)


def solution(mesh):
    in_specs = (
        P(("groups", "seq"), None),
        P(("groups", "seq"), None),
        P(("groups", "seq")),
        P(),
        P(),
        P(),
        P(("groups", "seq"), None),
        P(("groups", "seq"), None),
        P(("groups", "seq"), None, None),
        P(("groups", "seq"), None),
    )
    out_specs = (P(("groups", "seq"), None), P(("groups", "seq"), None))
    return jax.shard_map(shards, mesh=mesh, in_specs=in_specs, out_specs=out_specs, check_vma=False)
```
